32 devices in a mesh: ctx: 8 (over z, x), tp: 4 (over y, core).
Axes of the slice: x: 2, y: 2, z: 4, core: 2. Of those that a mesh axis runs over, the one named last changes fastest.
Arguments:
- resid: bfloat16 [1024, 8192], P('ctx', 'tp'), may hold values from -64 to 64
- q_mr: bfloat16 [1024, 8192], P('ctx', 'tp'), may hold values from -4 to 4
- k_mr: bfloat16 [1024, 8192], P('ctx', 'tp'), may hold values from -4 to 4
- v_mr: bfloat16 [1024, 8192], P('ctx', 'tp'), may hold values from -4 to 4
- mr_taps: bfloat16 [512, 128], P('tp'), may hold values from -0.5 to 0.5
- norm_gain: bfloat16 [8192], P('tp'), may hold values from 0.099609375 to 1.8984375
- q_lr: bfloat16 [1024, 8192], P('ctx', 'tp'), may hold values from -4 to 4
- k_lr: bfloat16 [1024, 8192], P('ctx', 'tp'), may hold values from -4 to 4
- pole_rate: float32 [16, 512], P(None, 'tp'), may hold values from 0 to 1, as said below
- residue: float32 [16, 512], P(None, 'tp'), may hold values from -3 to 3
Outputs:
- mixed: bfloat16 [1024, 8192], P('ctx', 'tp')
- lr_out: bfloat16 [1024, 8192], P('ctx', 'tp')
The draws below stay inside these ranges and needn't reach their ends.
Inputs may be any that keep to these rules, and one draw needn't show every extreme that they name: `pole_rate`: every rate is positive.
All inputs are finite; a program needn't handle non-finite values.
Results may differ from the reference program's by a relative error of at most 0.0052.
Values may be sent and summed in bfloat16 or wider, within the bound.
No kernel may reach another device: no remote copies, remote signals or barrier semaphores. Data moves between devices by JAX's collectives and lax.ppermute only.
A program may use at most 128 MiB of HBM per device.

```python
import jax
import jax.numpy as jnp
from jax import lax

D = 8192
GROUP = 16
POLES = 16
FILT = 128
TOK_DEV = 128
TOKENS = 1024
GROUPS = 512


def draw_resid(key, part):
    first_key, second_key = jax.random.split(key)
    column_pos = (jnp.arange(D, dtype=jnp.float32) + 0.5) / D
    base = jnp.clip(jax.random.normal(first_key, (TOKENS, D), jnp.float32), -4.0, 4.0)
    row_scale = jnp.exp(jax.random.uniform(second_key, (TOKENS, 1), jnp.float32, jnp.log(0.3), jnp.log(3.0)))
    col_scale = 3.0 ** column_pos
    return (base * row_scale * col_scale[None, :]).astype(jnp.bfloat16)


def draw_pole_rate(key, part):
    mask_key, slow_key, fast_key = jax.random.split(key, 3)
    share = 0.5
    slow_mask = jax.random.uniform(mask_key, (POLES, GROUPS), jnp.float32) < share
    slow_rate = jnp.exp(jax.random.uniform(slow_key, (POLES, GROUPS), jnp.float32, jnp.log(0.05), jnp.log(2.0))) / TOKENS
    fast_rate = jnp.exp(jax.random.uniform(fast_key, (POLES, GROUPS), jnp.float32, jnp.log(0.02), jnp.log(0.1)))
    return jnp.where(slow_mask, slow_rate, fast_rate)


def levels(rng, extent, pieces, least, high):
    level = 1.0
    for position, shards_of in pieces:
        heights = jax.random.uniform(jax.random.fold_in(jax.random.fold_in(rng, 6), position), (shards_of,), jnp.float32, least / len(pieces), high / len(pieces))
        level = level * jnp.repeat(jnp.exp(heights), extent[position] // shards_of).reshape((-1,) + (1,) * (len(extent) - 1 - position))
    return level


def normal_values(own_key, extent, deviation, most, shards=(), kind=jnp.bfloat16):
    level = levels(own_key, extent, shards, -0.22, 0.18) if shards else 1.0
    values = jax.random.normal(own_key, extent, jnp.float32) * deviation * level
    return jnp.minimum(jnp.maximum(values, -most), most).astype(kind)


def setup_inputs(seed: int = 0) -> dict:
    key_of = jax.random.split(jax.random.key(seed), 11)
    return {
        "resid": draw_resid(jax.random.fold_in(key_of[10], 71), 0),
        "q_mr": normal_values(key_of[1], (TOKENS, D), 1.0, 4.0, ((0, 8), (1, 4))),
        "k_mr": normal_values(key_of[2], (TOKENS, D), 1.0, 4.0, ((0, 8), (1, 4))),
        "v_mr": normal_values(key_of[3], (TOKENS, D), 1.0, 4.0, ((0, 8), (1, 4))),
        "mr_taps": normal_values(key_of[4], (GROUPS, FILT), FILT ** -0.5, 0.5, ((0, 4),)),
        "norm_gain": jnp.clip(1.0 + 0.18 * jax.random.normal(key_of[5], (D,), jnp.float32), 0.099609375, 1.8984375).astype(jnp.bfloat16),
        "q_lr": normal_values(key_of[6], (TOKENS, D), 1.0, 4.0, ((0, 8), (1, 4))),
        "k_lr": normal_values(key_of[7], (TOKENS, D), 1.0, 4.0, ((0, 8), (1, 4))),
        "pole_rate": draw_pole_rate(jax.random.fold_in(key_of[10], 71), 0),
        "residue": normal_values(key_of[9], (POLES, GROUPS), 0.5, 3.0, ((1, 4),), jnp.float32),
    }


HIGHEST_MODE = lax.Precision.HIGHEST

def banded(vector, out_rows):
    length = vector.shape[-1]
    span_cols = out_rows + length - 1
    padding = jnp.zeros(vector.shape[:-1] + (span_cols + 1 - length,), vector.dtype)
    line = jnp.concatenate([vector, padding], axis=-1)
    tiled = jnp.tile(line, (1,) * (vector.ndim - 1) + (out_rows,))
    return tiled[..., :out_rows * span_cols].reshape(vector.shape[:-1] + (out_rows, span_cols))

def modal_tables(pole_rate, residue, tok_rows):
    weights_eff = residue * jnp.sqrt(-jnp.expm1(-2.0 * pole_rate))
    positions = jnp.arange(tok_rows, dtype=jnp.float32)
    powers = jnp.exp(-pole_rate[:, :, None] * positions)
    impulse = lax.optimization_barrier(jnp.sum(weights_eff[:, :, None] * powers, axis=0))
    square = banded(impulse[:, ::-1], tok_rows)[:, :, tok_rows - 1:]
    entry = weights_eff[:, :, None] * powers * jnp.exp(-pole_rate)[:, :, None]
    leaving = powers[:, :, ::-1]
    through = jnp.exp(-pole_rate * tok_rows)
    return (square, entry, leaving, through)

def reference(resid, q_mr, k_mr, v_mr, mr_taps, norm_gain, q_lr, k_lr, pole_rate, residue):
    blocks = TOKENS // TOK_DEV
    window_len = TOK_DEV + FILT - 1
    mr_in = (k_mr.astype(jnp.float32) * v_mr.astype(jnp.float32)).astype(jnp.bfloat16)
    kernel = banded(mr_taps[:, ::-1], TOK_DEV).astype(jnp.float32)
    padded = jnp.concatenate([jnp.zeros((FILT - 1, D), jnp.bfloat16), mr_in], axis=0)

    def mr_block(block):
        start = (block * TOK_DEV).astype(jnp.int32)
        window = lax.dynamic_slice_in_dim(padded, start, window_len, 0)
        window = window.astype(jnp.float32).reshape(window_len, GROUPS, GROUP)
        return jnp.einsum('gtr,rgc->tgc', kernel, window).reshape(TOK_DEV, D)
    mr_conv = lax.map(mr_block, jnp.arange(blocks, dtype=jnp.int32)).reshape(TOKENS, D)
    mixed = (resid.astype(jnp.float32) + q_mr.astype(jnp.float32) * mr_conv).astype(jnp.bfloat16)
    mixed_f = mixed.astype(jnp.float32)
    mean_square = lax.optimization_barrier(jnp.mean(mixed_f * mixed_f, axis=1, keepdims=True))
    normed = mixed_f * lax.rsqrt(mean_square + 1e-06) * norm_gain.astype(jnp.float32)
    lr_in = k_lr.astype(jnp.float32) * normed
    square, entry, leaving, through = modal_tables(pole_rate, residue, TOK_DEV)
    blocks_in = lr_in.reshape(blocks, TOK_DEV, GROUPS, GROUP)

    def lr_step(carried, block_in):
        local = jnp.einsum('gts,sgc->tgc', square, block_in, precision=HIGHEST_MODE)
        incoming = jnp.einsum('pgt,pgc->tgc', entry, carried, precision=HIGHEST_MODE)
        state_end = jnp.einsum('pgs,sgc->pgc', leaving, block_in, precision=HIGHEST_MODE)
        return (through[:, :, None] * carried + state_end, local + incoming)
    start_state = jnp.zeros((POLES, GROUPS, GROUP), jnp.float32)
    _, conv_blocks = lax.scan(lr_step, start_state, blocks_in)
    lr_conv = conv_blocks.reshape(TOKENS, D)
    lr_out = (q_lr.astype(jnp.float32) * lr_conv).astype(jnp.bfloat16)
    return (mixed, lr_out)
```

```python
import functools

import jax
import jax.numpy as jnp
from jax import lax
from jax.experimental import pallas as pl
from jax.experimental.pallas import tpu as pltpu
from jax.sharding import PartitionSpec as P

LANES = 128
F32, BF16 = jnp.float32, jnp.bfloat16
VMEM = pl.BlockSpec(memory_space=pltpu.VMEM)


def shifted(x, axis, by):
    peers = lax.axis_size(axis)
    return lax.ppermute(x, axis, [(i, i + by) for i in range(peers) if i + by < peers])


def swapped(x, axis, bit):
    peers = lax.axis_size(axis)
    return lax.ppermute(x, axis, [(i, i ^ bit) for i in range(peers) if i ^ bit < peers])


def everyone(x, axis):
    peers = lax.axis_size(axis)
    if peers & (peers - 1) == 0:
        return [x] + [swapped(x, axis, bit) for bit in range(1, peers)]
    turns = [[(i, (i + by) % peers) for i in range(peers)] for by in range(1, peers)]
    return [x] + [lax.ppermute(x, axis, turn) for turn in turns]


def lane_group(shape, width):
    return lax.broadcasted_iota(jnp.int32, shape, 1) // width


def by_parity(x, group_size):
    odd = jnp.where(lane_group((1, LANES), group_size) % 2 == 1, 1.0, 0.0)
    return jnp.concatenate([x * (1.0 - odd).astype(x.dtype), x * odd.astype(x.dtype)], axis=0)


def own_lanes(stacked, group_size):
    pairs = LANES // (2 * group_size)
    rows = stacked.shape[0] // pairs
    pair_of = lane_group((rows, LANES), 2 * group_size)
    out = stacked[:rows]
    for pair in range(1, pairs):
        out = jnp.where(pair_of == pair, stacked[pair * rows : (pair + 1) * rows], out)
    return out


def matmul(a, b):
    return jnp.dot(a, b, preferred_element_type=F32)


def turned(row, size):
    return pltpu.roll(jnp.broadcast_to(row, (size, size)), 0, 1, stride=1, stride_axis=0)


def over_tiles(channels, body, init=0):
    return lax.fori_loop(0, channels // LANES, body, init)


def tile_of(i):
    return pl.ds(pl.multiple_of(i * LANES, LANES), LANES)


def prep_kernel(
    group_size, u_ref, taps_ref, rate_ref, weight_ref,
    acc_ref, upper_ref, square_ref, leave_ref, entry_ref, rev, lhs, enter,
):
    tok, channels = u_ref.shape
    poles, groups = rate_ref.shape
    per = LANES // group_size
    row = lax.broadcasted_iota(jnp.int32, (tok, tok), 0)
    col = lax.broadcasted_iota(jnp.int32, (tok, tok), 1)
    total = row + col
    flip = jnp.where((total == 0) | (total == tok), 1.0, 0.0).astype(BF16)
    rev[...] = matmul(taps_ref[...], flip)
    position = lax.broadcasted_iota(jnp.int32, (poles, tok), 1)
    back = jnp.where(position == 0, 0, tok - position).astype(F32)
    ahead = (position + 1).astype(F32)
    remain = (tok - 1 - position).astype(F32)

    def body(i, _):
        causal = row >= col
        turn = lax.rem(groups - i * per, groups)
        rate = pltpu.roll(rate_ref[...], turn, 1)
        weight = pltpu.roll(weight_ref[...], turn, 1)
        for k in range(per):
            pair, half = k // 2, k % 2
            rows, cols = pl.ds(pair * tok, tok), pl.ds(half * tok, tok)
            ring = turned(rev[pl.ds(i * per + k, 1), :], tok)
            lhs[rows, cols] = jnp.where(causal, ring, 0.0).astype(BF16)
            upper_ref[i, rows, cols] = jnp.where(causal, 0.0, ring).astype(BF16)
            rate_k = jnp.broadcast_to(rate[:, k : k + 1], (poles, tok))
            weight_k = jnp.broadcast_to(weight[:, k : k + 1], (poles, tok))
            impulse = jnp.sum(weight_k * jnp.exp(-rate_k * back), axis=0, keepdims=True)
            ring = turned(impulse, tok)
            square_ref[i, rows, cols] = jnp.where(causal, ring, 0.0).astype(BF16)
            leave_ref[i, pl.ds(pair * poles, poles), cols] = jnp.exp(-rate_k * remain)
            enter[pl.ds(k * poles, poles), :] = weight_k * jnp.exp(-rate_k * ahead)
        entry_ref[i] = enter[...].T.astype(BF16)
        x = by_parity(u_ref[:, tile_of(i)], group_size)
        acc_ref[:, tile_of(i)] = own_lanes(matmul(lhs[...], x), group_size)
        return 0

    over_tiles(channels, body)


def mix_kernel(
    group_size, halo_ref, acc_ref, upper_ref, resid_ref, q_ref, k_ref, gain_ref,
    mixed_ref, z_ref, zb_ref, sum_ref,
):
    tok, channels = halo_ref.shape

    def body(i, total):
        at = tile_of(i)
        past = own_lanes(matmul(upper_ref[i], by_parity(halo_ref[:, at], group_size)), group_size)
        conv = acc_ref[:, at] + past
        mixed = (resid_ref[:, at].astype(F32) + q_ref[:, at].astype(F32) * conv).astype(BF16)
        mixed_ref[:, at] = mixed
        mixed = mixed.astype(F32)
        z = k_ref[:, at].astype(F32) * mixed * gain_ref[:, at].astype(F32)
        z_ref[:, at] = z
        zb_ref[i] = by_parity(z.astype(BF16), group_size)
        return total + mixed * mixed

    total = over_tiles(channels, body, jnp.zeros((tok, LANES), F32))
    sum_ref[...] = jnp.sum(total.T, axis=0, keepdims=True)


def state_kernel(group_size, width, parts, *refs):
    sums, (leave_ref, zb_ref, state_ref, scale_ref) = refs[:parts], refs[parts:]
    square_sum = sums[0][...]
    for other in sums[1:]:
        square_sum = square_sum + other[...]
    scale = lax.rsqrt(square_sum / width + 1e-06)
    scale_ref[...] = scale
    twice = jnp.concatenate([scale, scale], axis=1)
    channels = state_ref.shape[1]

    def body(i, _):
        leaving = (leave_ref[i] * twice).astype(BF16)
        state_ref[:, tile_of(i)] = own_lanes(matmul(leaving, zb_ref[i]), group_size)
        return 0

    over_tiles(channels, body)


def local_kernel(group_size, scale_ref, z_ref, square_ref, local_ref):
    tok, channels = z_ref.shape
    scale = jnp.broadcast_to(scale_ref[...], (LANES, tok)).T

    def body(i, _):
        y = by_parity((z_ref[:, tile_of(i)] * scale).astype(BF16), group_size)
        local_ref[:, tile_of(i)] = own_lanes(matmul(square_ref[i], y), group_size)
        return 0

    over_tiles(channels, body)


def final_kernel(group_size, rounds, *refs):
    got, factors = refs[:rounds], refs[rounds : 2 * rounds]
    entry_ref, local_ref, q_ref, out_ref = refs[2 * rounds :]
    poles, channels = got[0].shape
    per = LANES // group_size
    group_of = lane_group((poles, LANES), group_size)

    def body(i, _):
        at = tile_of(i)
        carried = jnp.zeros((poles, LANES), F32)
        for state, factor in zip(got, factors):
            carried = carried + factor[:, at] * state[:, at].astype(F32)
        spread = jnp.concatenate([jnp.where(group_of == g, carried, 0.0) for g in range(per)], axis=0)
        conv = local_ref[:, at] + matmul(entry_ref[i], spread.astype(BF16))
        out_ref[:, at] = (q_ref[:, at].astype(F32) * conv).astype(BF16)
        return 0

    over_tiles(channels, body)


def held(shape, dtype):
    return jax.ShapeDtypeStruct(shape, dtype)


def call(kernel, outs, scratch, flops, *args):
    size = sum(a.size * a.dtype.itemsize for a in args)
    return pl.pallas_call(
        kernel,
        out_shape=outs,
        in_specs=[VMEM] * len(args),
        out_specs=jax.tree.map(lambda _: VMEM, outs),
        scratch_shapes=scratch,
        cost_estimate=pl.CostEstimate(flops=flops, bytes_accessed=size, transcendentals=0),
    )(*args)


def per_device(resid, q_mr, k_mr, v_mr, mr_taps, norm_gain, q_lr, k_lr, pole_rate, residue):
    tok, channels = resid.shape
    groups, tap_count = mr_taps.shape
    poles = pole_rate.shape[0]
    group_size = channels // groups
    assert tap_count == tok and channels % LANES == 0 and LANES % (2 * group_size) == 0
    tiles, pairs = channels // LANES, LANES // (2 * group_size)
    width = channels * lax.axis_size("tp")
    shards = lax.axis_size("ctx")
    place = lax.axis_index("ctx")
    bits = [1 << b for b in range((shards - 1).bit_length())]
    stacked = (tiles, pairs * tok, 2 * tok)
    work = 2 * tok * tok * channels * pairs * 2

    u = (k_mr.astype(F32) * v_mr.astype(F32)).astype(BF16)
    halo = shifted(u, "ctx", 1)

    weights = residue * jnp.sqrt(-jnp.expm1(-2.0 * pole_rate))
    acc, upper, square, leave, entry = call(
        functools.partial(prep_kernel, group_size),
        (
            held((tok, channels), F32),
            held(stacked, BF16),
            held(stacked, BF16),
            held((tiles, pairs * poles, 2 * tok), F32),
            held((tiles, tok, LANES // group_size * poles), BF16),
        ),
        [
            pltpu.VMEM((groups, tok), F32),
            pltpu.VMEM(stacked[1:], BF16),
            pltpu.VMEM((LANES // group_size * poles, tok), F32),
        ],
        4 * work,
        u, mr_taps, pole_rate, weights,
    )
    rate = jnp.repeat(pole_rate, group_size, axis=1) * tok
    factors, keeps, takes = [], [], []
    for bit in bits:
        late = (place & bit) != 0
        behind = (place & (bit - 1)).astype(F32)
        factors.append(jnp.where(late, jnp.exp(-rate * behind), 0.0))
        whole = jnp.exp(-rate * bit)
        keeps.append(jnp.where(late, 1.0, whole))
        takes.append(jnp.where(late, whole, 1.0))

    mixed, z, zb, square_sum = call(
        functools.partial(mix_kernel, group_size),
        (
            held((tok, channels), BF16),
            held((tok, channels), F32),
            held((tiles, 2 * tok, LANES), BF16),
            held((1, tok), F32),
        ),
        [],
        work,
        halo, acc, upper, resid, q_mr, k_lr, norm_gain.reshape(1, channels),
    )
    sums = everyone(square_sum, "tp")
    state, scale = call(
        functools.partial(state_kernel, group_size, width, len(sums)),
        (held((poles, channels), F32), held((1, tok), F32)),
        [],
        work // 8,
        *sums, leave, zb,
    )
    local = call(
        functools.partial(local_kernel, group_size),
        held((tok, channels), F32),
        [],
        work,
        scale, z, square,
    )
    got = []
    for step, bit in enumerate(bits):
        got.append(swapped(state.astype(BF16), "ctx", bit))
        state = keeps[step] * state + takes[step] * got[step].astype(F32)
    lr_out = call(
        functools.partial(final_kernel, group_size, len(bits)),
        held((tok, channels), BF16),
        [],
        work // 8,
        *got, *factors, entry, local, q_lr,
    )
    return (mixed, lr_out)


def solution(mesh):
    whole, tables = P("ctx", "tp"), P(None, "tp")
    placed = (whole,) * 4 + (P("tp", None), P("tp")) + (whole,) * 2 + (tables,) * 2
    return jax.shard_map(
        per_device, mesh=mesh, in_specs=placed, out_specs=(whole, whole), check_vma=False
    )
```

```python
import functools

import jax
import jax.numpy as jnp
from jax import lax
from jax.experimental import pallas as pl
from jax.experimental.pallas import tpu as pltpu
from jax.sharding import PartitionSpec as P

LANES = 128
GRANT = 16 << 20
F32, BF16 = jnp.float32, jnp.bfloat16
VMEM = pl.BlockSpec(memory_space=pltpu.VMEM)
SMEM = pl.BlockSpec(memory_space=pltpu.SMEM)
HBM = pl.BlockSpec(memory_space=pltpu.HBM)
PARTS = 4
SPAN = 16


def shifted(x, axis, by):
    peers = lax.axis_size(axis)
    return lax.ppermute(x, axis, [(i, i + by) for i in range(peers) if i + by < peers])


def swapped(x, axis, bit):
    peers = lax.axis_size(axis)
    return lax.ppermute(x, axis, [(i, i ^ bit) for i in range(peers) if i ^ bit < peers])


def everyone(x, axis):
    peers = lax.axis_size(axis)
    if peers & (peers - 1) == 0:
        return [x] + [swapped(x, axis, bit) for bit in range(1, peers)]
    turns = [[(i, (i + by) % peers) for i in range(peers)] for by in range(1, peers)]
    return [x] + [lax.ppermute(x, axis, turn) for turn in turns]


def lane_group(shape, width):
    return lax.broadcasted_iota(jnp.int32, shape, 1) // width


def by_parity(x, group_size):
    odd = jnp.where(lane_group((1, LANES), group_size) % 2 == 1, 1.0, 0.0)
    return jnp.concatenate([x * (1.0 - odd).astype(x.dtype), x * odd.astype(x.dtype)], axis=0)


def own_lanes(stacked, group_size):
    pairs = LANES // (2 * group_size)
    rows = stacked.shape[0] // pairs
    pair_of = lane_group((rows, LANES), 2 * group_size)
    out = stacked[:rows]
    for pair in range(1, pairs):
        out = jnp.where(pair_of == pair, stacked[pair * rows : (pair + 1) * rows], out)
    return out


def matmul(a, b):
    return jnp.dot(a, b, preferred_element_type=F32)


def pair_product(x, table, group_size):
    out = matmul(x, table)
    tok = out.shape[1] // 2
    return jnp.concatenate([out[:group_size, :tok], out[group_size:, tok:]], axis=0)


def turned(row, size):
    ring = pltpu.roll(jnp.broadcast_to(row, (size, size)), 0, 1, stride=1, stride_axis=0)
    return ring.astype(BF16)


def tile_of(i):
    return pl.ds(pl.multiple_of(i * LANES, LANES), LANES)


def spans(channels):
    size = max(LANES, channels // PARTS)
    return [pl.ds(start, size) for start in range(0, channels, size)]


def gate_kernel(k_hbm, v_hbm, out_ref, k_ref, v_ref, k_sem, v_sem):
    parts = spans(k_ref.shape[1])
    copies = []
    for n, at in enumerate(parts):
        copies.append(pltpu.make_async_copy(k_hbm.at[:, at], k_ref.at[:, at], k_sem.at[n]))
        copies.append(pltpu.make_async_copy(v_hbm.at[:, at], v_ref.at[:, at], v_sem.at[n]))
    for copy in copies:
        copy.start()
    for n, part in enumerate(parts):
        copies[2 * n].wait()
        copies[2 * n + 1].wait()
        for start in range(part.start, part.start + part.size, LANES):
            at = pl.ds(start, LANES)
            u = (k_ref[:, at].astype(F32) * v_ref[:, at].astype(F32)).astype(BF16)
            out_ref[at, :] = u.T


def prep_kernel(
    group_size, bits, place_ref, u_ref, weight_ref, gain_hbm, taps_hbm, rate_hbm, resid_hbm, q_hbm, k_hbm,
    base_ref, gate_ref, key_ref, upper_ref, square_ref, leave_ref, entry_ref, factor_ref, keep_ref, take_ref,
    taps, impulse, rates, weights, lower_ref, gain_ref, taps_ref, rate_ref, resid_ref, q_ref, k_ref, sems,
):
    channels, tok = u_ref.shape
    poles, groups = rate_ref.shape
    per, width = LANES // group_size, 2 * group_size
    sources = (taps_hbm, rate_hbm, gain_hbm, resid_hbm, q_hbm, k_hbm)
    places = (taps_ref, rate_ref, gain_ref, resid_ref, q_ref, k_ref)
    copies = [pltpu.make_async_copy(a, b, sems.at[n]) for n, (a, b) in enumerate(zip(sources, places))]
    for copy in copies:
        copy.start()
    row = lax.broadcasted_iota(jnp.int32, (tok, tok), 0)
    col = lax.broadcasted_iota(jnp.int32, (tok, tok), 1)
    causal = jnp.where(row <= col, 1.0, 0.0).astype(BF16)
    future = jnp.where(row <= col, 0.0, 1.0).astype(BF16)

    copies[0].wait()
    taps[...] = taps_ref[...].astype(F32)

    def taps_tables(i, _):
        for k in range(SPAN):
            ring = turned(taps[pl.ds(i * SPAN + k, 1), :], tok)
            at, cols = i * (SPAN // 2) + k // 2, pl.ds(k % 2 * tok, tok)
            lower_ref[at, :, cols] = ring * causal
            upper_ref[at, :, cols] = ring * future
        return 0

    lax.fori_loop(0, groups // SPAN, taps_tables, 0)

    copies[1].wait()
    for g in range(groups):
        at = pl.ds(g * poles, poles)
        rates[at, :] = jnp.broadcast_to(rate_ref[:, g : g + 1], (poles, tok))
        weights[at, :] = jnp.broadcast_to(weight_ref[:, g : g + 1], (poles, tok))

    position = lax.broadcasted_iota(jnp.int32, (poles, tok), 1)
    now = position.astype(F32)
    ahead = (position + 1).astype(F32)
    remain = (tok - 1 - position).astype(F32)
    place = place_ref[0]
    lane_of = lane_group((poles, LANES), group_size)

    def decays(i, _):
        spread = jnp.zeros((poles, LANES), F32)
        for k in range(per):
            at = pl.ds(pl.multiple_of((i * per + k) * poles, poles), poles)
            rate, weight = rates[at, :], weights[at, :]
            impulse[pl.ds(i * per + k, 1), :] = jnp.sum(weight * jnp.exp(-rate * now), axis=0, keepdims=True)
            leave_ref[i, pl.ds(k // 2 * poles, poles), pl.ds(k % 2 * tok, tok)] = jnp.exp(-rate * remain)
            weights[at, :] = weight * jnp.exp(-rate * ahead)
            spread = jnp.where(lane_of == k, rate, spread)
        spread = spread * tok
        at = tile_of(i)
        for step, bit in enumerate(bits):
            late = (place & bit) != 0
            behind = (place & (bit - 1)).astype(F32)
            whole = jnp.exp(-spread * bit)
            factor_ref[step, :, at] = jnp.where(late, jnp.exp(-spread * behind), 0.0)
            keep_ref[step, :, at] = jnp.where(late, 1.0, whole)
            take_ref[step, :, at] = jnp.where(late, whole, 1.0)
        return 0

    lax.fori_loop(0, channels // LANES, decays, 0, unroll=2)

    def square_tables(i, _):
        for k in range(SPAN):
            ring = turned(impulse[pl.ds(i * SPAN + k, 1), :], tok)
            square_ref[i * (SPAN // 2) + k // 2, :, pl.ds(k % 2 * tok, tok)] = ring * causal
        return 0

    lax.fori_loop(0, groups // SPAN, square_tables, 0)

    for pair in range(channels // width):
        at = pl.ds(pair * width, width)
        base_ref[at, :] = pair_product(u_ref[at, :], lower_ref[pair], group_size)

    for copy in copies[2:]:
        copy.wait()
    for i in range(channels // LANES):
        at = pl.ds(i * LANES, LANES)
        gate = q_ref[:, at].T.astype(F32)
        gate_ref[at, :] = gate
        base_ref[at, :] = resid_ref[:, at].T.astype(F32) + gate * base_ref[at, :]
        key_ref[at, :] = (k_ref[:, at].astype(F32) * gain_ref[i : i + 1, :].astype(F32)).T
        entry = weights[pl.ds(i * per * poles, per * poles), :].T
        high = entry.astype(BF16)
        entry_ref[i, :, :LANES] = high
        entry_ref[i, :, LANES:] = (entry - high.astype(F32)).astype(BF16)


def mix_kernel(group_size, halo_ref, upper_ref, base_ref, gate_ref, key_ref, mixed_ref, z_ref, sum_ref):
    channels, tok = halo_ref.shape
    width = 2 * group_size
    total = jnp.zeros((width, tok), F32)
    for pair in range(channels // width):
        at = pl.ds(pair * width, width)
        past = pair_product(halo_ref[at, :], upper_ref[pair], group_size)
        mixed = (base_ref[at, :] + gate_ref[at, :] * past).astype(BF16)
        mixed_ref[at, :] = mixed
        mixed = mixed.astype(F32)
        z_ref[at, :] = key_ref[at, :] * mixed
        total = total + mixed * mixed
    sum_ref[...] = jnp.sum(total, axis=0, keepdims=True)


def turn_kernel(group_size, z_ref, zb_ref):
    for i in range(z_ref.shape[0] // LANES):
        zb_ref[i] = by_parity(z_ref[pl.ds(i * LANES, LANES), :].astype(BF16).T, group_size)


def written(tile, out_hbm, out_ref, sem):
    copies = []
    for n, part in enumerate(spans(out_ref.shape[1])):
        for start in range(part.start, part.start + part.size, LANES):
            out_ref[:, pl.ds(start, LANES)] = tile(start // LANES)
        copies.append(pltpu.make_async_copy(out_ref.at[:, part], out_hbm.at[:, part], sem.at[n]))
        copies[-1].start()
    for copy in copies:
        copy.wait()


def out_kernel(mixed_ref, out_hbm, out_ref, sem):
    written(lambda i: mixed_ref[pl.ds(i * LANES, LANES), :].T, out_hbm, out_ref, sem)


def state_kernel(group_size, width, parts, *refs):
    sums, (leave_ref, zb_ref, state_ref, sent_ref, scale_ref) = refs[:parts], refs[parts:]
    square_sum = sums[0][...]
    for other in sums[1:]:
        square_sum = square_sum + other[...]
    scale = lax.rsqrt(square_sum / width + 1e-06)
    scale_ref[...] = scale
    twice = jnp.concatenate([scale, scale], axis=1)
    for i in range(leave_ref.shape[0]):
        at = pl.ds(i * LANES, LANES)
        leaving = (leave_ref[i] * twice).astype(BF16)
        state = own_lanes(matmul(leaving, zb_ref[i]), group_size)
        state_ref[:, at] = state
        sent_ref[:, at] = state.astype(BF16)


def local_kernel(group_size, scale_ref, z_ref, square_ref, local_ref):
    channels, tok = z_ref.shape
    width = 2 * group_size
    scale = scale_ref[...]

    def body(i, _):
        rows = []
        for pair in range(LANES // width):
            at = pl.ds(pl.multiple_of(i * LANES + pair * width, width), width)
            y = (z_ref[at, :] * scale).astype(BF16)
            rows.append(pair_product(y, square_ref[i * (LANES // width) + pair], group_size))
        local_ref[:, tile_of(i)] = jnp.concatenate(rows, axis=0).T
        return 0

    lax.fori_loop(0, channels // LANES, body, 0, unroll=4)


def final_kernel(group_size, rounds, *refs):
    got, (factor_ref, entry_ref, local_ref, q_ref, out_hbm, out_ref, sem) = refs[:rounds], refs[rounds:]
    poles, channels = got[0].shape
    per = LANES // group_size
    group_of = lane_group((poles, LANES), group_size)

    def tile(i):
        at = pl.ds(i * LANES, LANES)
        carried = factor_ref[0, :, at] * got[0][:, at].astype(F32)
        for step in range(1, rounds):
            carried = carried + factor_ref[step, :, at] * got[step][:, at].astype(F32)
        spread = [jnp.where(group_of == g, carried, 0.0).astype(BF16) for g in range(per)]
        conv = local_ref[:, at] + matmul(entry_ref[i], jnp.concatenate(spread * 2, axis=0))
        return (q_ref[:, at].astype(F32) * conv).astype(BF16)

    written(tile, out_hbm, out_ref, sem)


def held(shape, dtype):
    return jax.ShapeDtypeStruct(shape, dtype)


def call(kernel, outs, scratch, flops, *args, **more):
    size = sum(a.size * a.dtype.itemsize for a in args)
    places = more.get("in_specs", [VMEM] * len(args))
    args = [pltpu.with_memory_space_constraint(a, pltpu.HBM) if s is HBM else a for a, s in zip(args, places)]
    options = dict(
        in_specs=[VMEM] * len(args), out_specs=jax.tree.map(lambda _: VMEM, outs), scratch_shapes=scratch
    )
    return pl.pallas_call(
        kernel,
        out_shape=outs,
        cost_estimate=pl.CostEstimate(flops=flops, bytes_accessed=size, transcendentals=0),
        compiler_params=pltpu.CompilerParams(vmem_limit_bytes=GRANT),
        **{**options, **more},
    )(*args)


def per_device(resid, q_mr, k_mr, v_mr, mr_taps, norm_gain, q_lr, k_lr, pole_rate, residue):
    tok, channels = resid.shape
    groups, tap_count = mr_taps.shape
    poles = pole_rate.shape[0]
    group_size = channels // groups
    assert tap_count == tok and channels % LANES == 0 and LANES % (2 * group_size) == 0
    tiles, per = channels // LANES, LANES // group_size
    shards = lax.axis_size("ctx")
    bits = [1 << b for b in range((shards - 1).bit_length())]
    rounds = len(bits)
    place = lax.axis_index("ctx").astype(jnp.int32).reshape(1)
    work = 4 * tok * tok * channels

    rows = pltpu.VMEM((tok, channels), BF16)
    sem = pltpu.SemaphoreType.DMA((PARTS,))
    u = call(
        gate_kernel, held((channels, tok), BF16), [rows, rows, sem, sem], work // 8, k_mr, v_mr,
        in_specs=[HBM, HBM],
    )
    halo = shifted(u, "ctx", 1)

    weights = residue * jnp.sqrt(-jnp.expm1(-2.0 * pole_rate))
    tall = held((channels, tok), F32)
    table = held((groups // 2, tok, 2 * tok), BF16)
    steps = held((rounds, poles, channels), F32)
    base, gate, key, upper, square, leave, entry, factor, keep, take = call(
        functools.partial(prep_kernel, group_size, bits),
        (
            tall, tall, tall, table, table,
            held((tiles, per // 2 * poles, 2 * tok), F32),
            held((tiles, tok, 2 * per * poles), BF16),
            steps, steps, steps,
        ),
        [
            pltpu.VMEM((groups, tok), F32), pltpu.VMEM((groups, tok), F32), pltpu.VMEM((groups * poles, tok), F32),
            pltpu.VMEM((groups * poles, tok), F32), pltpu.VMEM(table.shape, BF16), pltpu.VMEM((tiles, LANES), BF16),
            pltpu.VMEM((groups, tok), BF16), pltpu.VMEM((poles, groups), F32), rows, rows, rows,
            pltpu.SemaphoreType.DMA((6,)),
        ],
        8 * work,
        place, u, weights, norm_gain.reshape(tiles, LANES), mr_taps, pole_rate, resid, q_mr, k_lr,
        in_specs=[SMEM, VMEM, VMEM] + [HBM] * 6,
    )
    mixed_t, z, square_sum = call(
        functools.partial(mix_kernel, group_size),
        (held((channels, tok), BF16), tall, held((1, tok), F32)),
        [],
        work,
        halo, upper, base, gate, key,
    )
    sums = everyone(square_sum, "tp")
    zb = call(
        functools.partial(turn_kernel, group_size), held((tiles, 2 * tok, LANES), BF16), [], work // 2, z
    )
    small = (poles, channels)
    state, sent, scale = call(
        functools.partial(state_kernel, group_size, channels * lax.axis_size("tp"), len(sums)),
        (held(small, F32), held(small, BF16), held((1, tok), F32)),
        [],
        work // 8,
        *sums, leave, zb,
    )
    local = call(
        functools.partial(local_kernel, group_size),
        held((tok, channels), F32),
        [],
        work,
        scale, z, square,
    )
    got = []
    for step, bit in enumerate(bits):
        got.append(swapped(sent, "ctx", bit))
        state = keep[step] * state + take[step] * got[step].astype(F32)
        sent = state.astype(BF16)
    mixed = call(out_kernel, held((tok, channels), BF16), [rows, sem], work // 4, mixed_t, out_specs=HBM)
    lr_out = call(
        functools.partial(final_kernel, group_size, rounds),
        held((tok, channels), BF16),
        [rows, sem],
        work // 8,
        *got, factor, entry, local, q_lr,
        out_specs=HBM,
    )
    return (mixed, lr_out)


def solution(mesh):
    whole, tables = P("ctx", "tp"), P(None, "tp")
    placed = (whole,) * 4 + (P("tp", None), P("tp")) + (whole,) * 2 + (tables,) * 2
    return jax.shard_map(
        per_device, mesh=mesh, in_specs=placed, out_specs=(whole, whole), check_vma=False
    )
```

```python
import functools

import jax
import jax.numpy as jnp
from jax import lax
from jax.experimental import pallas as pl
from jax.experimental.pallas import tpu as pltpu
from jax.sharding import PartitionSpec as P

LANES = 128
GRANT = 16 << 20
F32, BF16 = jnp.float32, jnp.bfloat16
VMEM = pl.BlockSpec(memory_space=pltpu.VMEM)
SMEM = pl.BlockSpec(memory_space=pltpu.SMEM)
HBM = pl.BlockSpec(memory_space=pltpu.HBM)
PARTS = 4
CHUNKS = 2
SMALL, TERMS = 0.5, 10
SPAN = 16


def shifted(x, axis, by):
    peers = lax.axis_size(axis)
    return lax.ppermute(x, axis, [(i, i + by) for i in range(peers) if i + by < peers])


def swapped(x, axis, bit):
    peers = lax.axis_size(axis)
    return lax.ppermute(x, axis, [(i, i ^ bit) for i in range(peers) if i ^ bit < peers])


def everyone(x, axis):
    peers = lax.axis_size(axis)
    if peers & (peers - 1) == 0:
        return [x] + [swapped(x, axis, bit) for bit in range(1, peers)]
    turns = [[(i, (i + by) % peers) for i in range(peers)] for by in range(1, peers)]
    return [x] + [lax.ppermute(x, axis, turn) for turn in turns]


def lane_group(shape, width):
    return lax.broadcasted_iota(jnp.int32, shape, 1) // width


def by_parity(x, group_size):
    odd = jnp.where(lane_group((1, LANES), group_size) % 2 == 1, 1.0, 0.0)
    return jnp.concatenate([x * (1.0 - odd).astype(x.dtype), x * odd.astype(x.dtype)], axis=0)


def own_lanes(stacked, group_size):
    pairs = LANES // (2 * group_size)
    rows = stacked.shape[0] // pairs
    pair_of = lane_group((rows, LANES), 2 * group_size)
    out = stacked[:rows]
    for pair in range(1, pairs):
        out = jnp.where(pair_of == pair, stacked[pair * rows : (pair + 1) * rows], out)
    return out


def matmul(a, b):
    return jnp.dot(a, b, preferred_element_type=F32)


def pair_product(x, table, group_size):
    out = matmul(x, table)
    tok = out.shape[1] // 2
    return jnp.concatenate([out[:group_size, :tok], out[group_size:, tok:]], axis=0)


def turned(row, size):
    ring = pltpu.roll(jnp.broadcast_to(row, (size, size)), 0, 1, stride=1, stride_axis=0)
    return ring.astype(BF16)


def series(x):
    out = jnp.ones_like(x)
    for n in range(TERMS, 1, -1):
        out = 1.0 - x / n * out
    return out


def tile_of(i):
    return pl.ds(pl.multiple_of(i * LANES, LANES), LANES)


def spans(channels):
    size = max(LANES, channels // PARTS)
    return [pl.ds(start, size) for start in range(0, channels, size)]


def gated(k, v, out_ref):
    for start in range(0, out_ref.shape[0], LANES):
        at = pl.ds(start, LANES)
        out_ref[at, :] = (k[:, at].astype(F32) * v[:, at].astype(F32)).astype(BF16).T


def first_kernel(k_hbm, v_hbm, out_ref, *refs):
    later, (k_ref, v_ref, sems) = refs[:-3], refs[-3:]
    chunk = out_ref.shape[0]
    copies = []
    for n, to in enumerate((k_ref, v_ref) + later):
        source = (k_hbm, v_hbm)[n % 2].at[:, pl.ds(n // 2 * chunk, chunk)]
        copies.append(pltpu.make_async_copy(source, to, sems.at[n]))
        copies[-1].start()
    copies[0].wait()
    copies[1].wait()
    gated(k_ref, v_ref, out_ref)
    for copy in copies[2:]:
        copy.wait()


def prep_kernel(
    group_size, bits, place_ref, u_refs, gain_hbm, taps_hbm, rate_hbm, residue_hbm, resid_hbm, q_hbm, k_hbm,
    base_ref, gate_ref, key_ref, upper_ref, square_ref, leave_ref, entry_ref, factor_ref, keep_ref, take_ref,
    taps, impulse, rates, weights, lower_ref,
    gain_ref, taps_ref, rate_ref, residue_ref, resid_ref, q_ref, k_ref, sems,
):
    chunk, tok = u_refs[0].shape
    channels = chunk * len(u_refs)
    poles, groups = rate_ref.shape
    per, width = LANES // group_size, 2 * group_size
    sources = (taps_hbm, rate_hbm, residue_hbm, gain_hbm, resid_hbm, q_hbm, k_hbm)
    places = (taps_ref, rate_ref, residue_ref, gain_ref, resid_ref, q_ref, k_ref)
    copies = [pltpu.make_async_copy(a, b, sems.at[n]) for n, (a, b) in enumerate(zip(sources, places))]
    for copy in copies:
        copy.start()
    row = lax.broadcasted_iota(jnp.int32, (tok, tok), 0)
    col = lax.broadcasted_iota(jnp.int32, (tok, tok), 1)
    causal = jnp.where(row <= col, 1.0, 0.0).astype(BF16)
    future = jnp.where(row <= col, 0.0, 1.0).astype(BF16)

    copies[0].wait()
    taps[...] = taps_ref[...].astype(F32)

    def taps_tables(i, _):
        for k in range(SPAN):
            ring = turned(taps[pl.ds(i * SPAN + k, 1), :], tok)
            at, cols = i * (SPAN // 2) + k // 2, pl.ds(k % 2 * tok, tok)
            lower_ref[at, :, cols] = ring * causal
            upper_ref[at, :, cols] = ring * future
        return 0

    lax.fori_loop(0, groups // SPAN, taps_tables, 0)

    copies[1].wait()
    copies[2].wait()
    twice = 2.0 * rate_ref[...]
    weight = residue_ref[...] * jnp.sqrt(jnp.where(twice < SMALL, twice * series(twice), 1.0 - jnp.exp(-twice)))
    for g in range(groups):
        at = pl.ds(g * poles, poles)
        rates[at, :] = jnp.broadcast_to(rate_ref[:, g : g + 1], (poles, tok))
        weights[at, :] = jnp.broadcast_to(weight[:, g : g + 1], (poles, tok))

    position = lax.broadcasted_iota(jnp.int32, (poles, tok), 1)
    now = position.astype(F32)
    ahead = (position + 1).astype(F32)
    remain = (tok - 1 - position).astype(F32)
    place = place_ref[0]
    lane_of = lane_group((poles, LANES), group_size)

    def decays(i, _):
        spread = jnp.zeros((poles, LANES), F32)
        for k in range(per):
            at = pl.ds(pl.multiple_of((i * per + k) * poles, poles), poles)
            rate, weight = rates[at, :], weights[at, :]
            impulse[pl.ds(i * per + k, 1), :] = jnp.sum(weight * jnp.exp(-rate * now), axis=0, keepdims=True)
            leave_ref[i, pl.ds(k // 2 * poles, poles), pl.ds(k % 2 * tok, tok)] = jnp.exp(-rate * remain)
            weights[at, :] = weight * jnp.exp(-rate * ahead)
            spread = jnp.where(lane_of == k, rate, spread)
        spread = spread * tok
        at = tile_of(i)
        for step, bit in enumerate(bits):
            late = (place & bit) != 0
            behind = (place & (bit - 1)).astype(F32)
            whole = jnp.exp(-spread * bit)
            factor_ref[step, :, at] = jnp.where(late, jnp.exp(-spread * behind), 0.0)
            keep_ref[step, :, at] = jnp.where(late, 1.0, whole)
            take_ref[step, :, at] = jnp.where(late, whole, 1.0)
        return 0

    lax.fori_loop(0, channels // LANES, decays, 0, unroll=2)

    def square_tables(i, _):
        for k in range(SPAN):
            ring = turned(impulse[pl.ds(i * SPAN + k, 1), :], tok)
            square_ref[i * (SPAN // 2) + k // 2, :, pl.ds(k % 2 * tok, tok)] = ring * causal
        return 0

    lax.fori_loop(0, groups // SPAN, square_tables, 0)

    for pair in range(channels // width):
        at = pl.ds(pair * width, width)
        u = u_refs[pair * width // chunk][pl.ds(pair * width % chunk, width), :]
        base_ref[at, :] = pair_product(u, lower_ref[pair], group_size)

    for copy in copies[3:]:
        copy.wait()
    for i in range(channels // LANES):
        at = pl.ds(i * LANES, LANES)
        gate = q_ref[:, at].T.astype(F32)
        gate_ref[at, :] = gate
        base_ref[at, :] = resid_ref[:, at].T.astype(F32) + gate * base_ref[at, :]
        key_ref[at, :] = (k_ref[:, at].astype(F32) * gain_ref[i : i + 1, :].astype(F32)).T
        entry = weights[pl.ds(i * per * poles, per * poles), :].T
        high = entry.astype(BF16)
        entry_ref[i, :, :LANES] = high
        entry_ref[i, :, LANES:] = (entry - high.astype(F32)).astype(BF16)


def mix_kernel(group_size, first, halo_ref, upper_ref, base_ref, gate_ref, key_ref, *refs):
    before, (mixed_ref, z_ref, sum_ref) = refs[:-3], refs[-3:]
    channels, tok = halo_ref.shape
    width = 2 * group_size
    total = jnp.zeros((width, tok), F32)
    for pair in range(channels // width):
        at, there = pl.ds(pair * width, width), pl.ds(first + pair * width, width)
        past = pair_product(halo_ref[at, :], upper_ref[first // width + pair], group_size)
        mixed = (base_ref[there, :] + gate_ref[there, :] * past).astype(BF16)
        mixed_ref[at, :] = mixed
        mixed = mixed.astype(F32)
        z_ref[at, :] = key_ref[there, :] * mixed
        total = total + mixed * mixed
    total = jnp.sum(total, axis=0, keepdims=True)
    for ref in before:
        total = total + ref[...]
    sum_ref[...] = total


def rows_of(refs, start, size):
    chunk = refs[0].shape[0]
    return refs[start // chunk][pl.ds(start % chunk, size), :]


def turn_kernel(group_size, z_refs, zb_ref):
    for i in range(zb_ref.shape[0]):
        zb_ref[i] = by_parity(rows_of(z_refs, i * LANES, LANES).astype(BF16).T, group_size)


def written(tile, out_hbm, out_ref, sem):
    copies = []
    for n, part in enumerate(spans(out_ref.shape[1])):
        for start in range(part.start, part.start + part.size, LANES):
            out_ref[:, pl.ds(start, LANES)] = tile(start // LANES)
        copies.append(pltpu.make_async_copy(out_ref.at[:, part], out_hbm.at[:, part], sem.at[n]))
        copies[-1].start()
    for copy in copies:
        copy.wait()


def out_kernel(mixed_refs, out_hbm, out_ref, sem):
    written(lambda i: rows_of(mixed_refs, i * LANES, LANES).T, out_hbm, out_ref, sem)


def state_kernel(group_size, width, parts, *refs):
    sums, (leave_ref, zb_ref, state_ref, sent_ref, scale_ref) = refs[:parts], refs[parts:]
    square_sum = sums[0][...]
    for other in sums[1:]:
        square_sum = square_sum + other[...]
    scale = lax.rsqrt(square_sum / width + 1e-06)
    scale_ref[...] = scale
    twice = jnp.concatenate([scale, scale], axis=1)
    for i in range(leave_ref.shape[0]):
        at = pl.ds(i * LANES, LANES)
        leaving = (leave_ref[i] * twice).astype(BF16)
        state = own_lanes(matmul(leaving, zb_ref[i]), group_size)
        state_ref[:, at] = state
        sent_ref[:, at] = state.astype(BF16)


def local_kernel(group_size, scale_ref, z_refs, square_ref, local_ref):
    chunk = z_refs[0].shape[0]
    width = 2 * group_size
    scale = scale_ref[...]
    for n, z_ref in enumerate(z_refs):

        def body(i, _):
            rows = []
            for pair in range(LANES // width):
                at = pl.ds(pl.multiple_of(i * LANES + pair * width, width), width)
                y = (z_ref[at, :] * scale).astype(BF16)
                table = square_ref[n * (chunk // width) + i * (LANES // width) + pair]
                rows.append(pair_product(y, table, group_size))
            local_ref[:, tile_of(n * (chunk // LANES) + i)] = jnp.concatenate(rows, axis=0).T
            return 0

        lax.fori_loop(0, chunk // LANES, body, 0, unroll=4)


def final_kernel(group_size, rounds, *refs):
    got, (factor_ref, entry_ref, local_ref, q_ref, out_hbm, out_ref, sem) = refs[:rounds], refs[rounds:]
    poles, channels = got[0].shape
    per = LANES // group_size
    group_of = lane_group((poles, LANES), group_size)

    def tile(i):
        at = pl.ds(i * LANES, LANES)
        carried = factor_ref[0, :, at] * got[0][:, at].astype(F32)
        for step in range(1, rounds):
            carried = carried + factor_ref[step, :, at] * got[step][:, at].astype(F32)
        spread = [jnp.where(group_of == g, carried, 0.0).astype(BF16) for g in range(per)]
        conv = local_ref[:, at] + matmul(entry_ref[i], jnp.concatenate(spread * 2, axis=0))
        return (q_ref[:, at].astype(F32) * conv).astype(BF16)

    written(tile, out_hbm, out_ref, sem)


def held(shape, dtype):
    return jax.ShapeDtypeStruct(shape, dtype)


def call(kernel, outs, scratch, flops, *args, **more):
    places = more.get("in_specs", [VMEM] * len(args))
    args = [pltpu.with_memory_space_constraint(a, pltpu.HBM) if s is HBM else a for a, s in zip(args, places)]
    specs = [[s] * len(a) if isinstance(a, list) else s for a, s in zip(args, places)]
    size = sum(a.size * a.dtype.itemsize for a in jax.tree.leaves(args))
    return pl.pallas_call(
        kernel,
        in_specs=specs,
        out_specs=more.get("out_specs", jax.tree.map(lambda _: VMEM, outs)),
        out_shape=outs,
        scratch_shapes=scratch,
        cost_estimate=pl.CostEstimate(flops=flops, bytes_accessed=size, transcendentals=0),
        compiler_params=pltpu.CompilerParams(vmem_limit_bytes=GRANT),
    )(*args)


def per_device(resid, q_mr, k_mr, v_mr, mr_taps, norm_gain, q_lr, k_lr, pole_rate, residue):
    tok, channels = resid.shape
    groups, tap_count = mr_taps.shape
    poles = pole_rate.shape[0]
    group_size = channels // groups
    assert tap_count == tok and channels % LANES == 0 and LANES % (2 * group_size) == 0
    tiles, per = channels // LANES, LANES // group_size
    shards = lax.axis_size("ctx")
    bits = [1 << b for b in range((shards - 1).bit_length())]
    rounds = len(bits)
    place = lax.axis_index("ctx").astype(jnp.int32).reshape(1)
    work = 4 * tok * tok * channels

    chunk = channels // CHUNKS
    firsts = range(0, channels, chunk)
    part = pltpu.VMEM((tok, chunk), BF16)
    rows = pltpu.VMEM((tok, channels), BF16)
    sem = pltpu.SemaphoreType.DMA((PARTS,))
    late = [held((tok, chunk), BF16)] * (2 * CHUNKS - 2)
    outs = call(
        first_kernel, [held((chunk, tok), BF16)] + late, [part, part, pltpu.SemaphoreType.DMA((2 * CHUNKS,))],
        work // 8, k_mr, v_mr, in_specs=[HBM, HBM],
    )
    u = [outs[0]]
    halo = [shifted(u[0], "ctx", 1)]
    for n in range(1, len(outs), 2):
        u.append(call(gated, held((chunk, tok), BF16), [], work // 8, *outs[n : n + 2]))
        halo.append(shifted(u[-1], "ctx", 1))

    tall = held((channels, tok), F32)
    table = held((groups // 2, tok, 2 * tok), BF16)
    steps = held((rounds, poles, channels), F32)
    base, gate, key, upper, square, leave, entry, factor, keep, take = call(
        functools.partial(prep_kernel, group_size, bits),
        (
            tall, tall, tall, table, table,
            held((tiles, per // 2 * poles, 2 * tok), F32),
            held((tiles, tok, 2 * per * poles), BF16),
            steps, steps, steps,
        ),
        [
            pltpu.VMEM((groups, tok), F32), pltpu.VMEM((groups, tok), F32), pltpu.VMEM((groups * poles, tok), F32),
            pltpu.VMEM((groups * poles, tok), F32), pltpu.VMEM(table.shape, BF16), pltpu.VMEM((tiles, LANES), BF16),
            pltpu.VMEM((groups, tok), BF16), pltpu.VMEM((poles, groups), F32), pltpu.VMEM((poles, groups), F32),
            rows, rows, rows, pltpu.SemaphoreType.DMA((7,)),
        ],
        8 * work,
        place, u, norm_gain.reshape(tiles, LANES), mr_taps, pole_rate, residue, resid, q_mr, k_lr,
        in_specs=[SMEM, VMEM] + [HBM] * 7,
    )
    mixed_t, z, square_sum = [], [], []
    for first, past in zip(firsts, halo):
        outs = call(
            functools.partial(mix_kernel, group_size, first),
            (held((chunk, tok), BF16), held((chunk, tok), F32), held((1, tok), F32)),
            [],
            work // CHUNKS,
            past, upper, base, gate, key, *square_sum,
        )
        mixed_t.append(outs[0])
        z.append(outs[1])
        square_sum = [outs[2]]
    square_sum = square_sum[0]
    sums = everyone(square_sum, "tp")
    zb = call(
        functools.partial(turn_kernel, group_size), held((tiles, 2 * tok, LANES), BF16), [], work // 2, z
    )
    small = (poles, channels)
    state, sent, scale = call(
        functools.partial(state_kernel, group_size, channels * lax.axis_size("tp"), len(sums)),
        (held(small, F32), held(small, BF16), held((1, tok), F32)),
        [],
        work // 8,
        *sums, leave, zb,
    )
    local = call(
        functools.partial(local_kernel, group_size),
        held((tok, channels), F32),
        [],
        work,
        scale, z, square,
    )
    got = []
    for step, bit in enumerate(bits):
        got.append(swapped(sent, "ctx", bit))
        state = keep[step] * state + take[step] * got[step].astype(F32)
        sent = state.astype(BF16)
    mixed = call(out_kernel, held((tok, channels), BF16), [rows, sem], work // 4, mixed_t, out_specs=HBM)
    lr_out = call(
        functools.partial(final_kernel, group_size, rounds),
        held((tok, channels), BF16),
        [rows, sem],
        work // 8,
        *got, factor, entry, local, q_lr,
        out_specs=HBM,
    )
    return (mixed, lr_out)


def solution(mesh):
    whole, tables = P("ctx", "tp"), P(None, "tp")
    placed = (whole,) * 4 + (P("tp", None), P("tp")) + (whole,) * 2 + (tables,) * 2
    return jax.shard_map(
        per_device, mesh=mesh, in_specs=placed, out_specs=(whole, whole), check_vma=False
    )
```

```python
import functools

import jax
import jax.numpy as jnp
from jax import lax
from jax.experimental import pallas as pl
from jax.experimental.pallas import tpu as pltpu
from jax.sharding import PartitionSpec as P


LANES = 128
GRANT = 16 << 20
F32, BF16 = jnp.float32, jnp.bfloat16
VMEM = pl.BlockSpec(memory_space=pltpu.VMEM)
SMEM = pl.BlockSpec(memory_space=pltpu.SMEM)
HBM = pl.BlockSpec(memory_space=pltpu.HBM)
PARTS = 4
FIRST = 8
SMALL, TERMS = 0.5, 10
SPAN = 16


def passed_on(x, close):
    shards = lax.axis_size("ctx")
    pairs = [(i, (i + 1) % shards) for i in range(shards if close else shards - 1)]
    return lax.ppermute(x, "ctx", pairs)


def swapped(x, axis, bit):
    peers = lax.axis_size(axis)
    return lax.ppermute(x, axis, [(i, i ^ bit) for i in range(peers) if i ^ bit < peers])


def everyone(x, axis):
    peers = lax.axis_size(axis)
    if peers & (peers - 1) == 0:
        return [x] + [swapped(x, axis, bit) for bit in range(1, peers)]
    turns = [[(i, (i + by) % peers) for i in range(peers)] for by in range(1, peers)]
    return [x] + [lax.ppermute(x, axis, turn) for turn in turns]


def lane_group(shape, width):
    return lax.broadcasted_iota(jnp.int32, shape, 1) // width


def by_parity(x, group_size):
    odd = jnp.where(lane_group((1, LANES), group_size) % 2 == 1, 1.0, 0.0)
    return jnp.concatenate([x * (1.0 - odd).astype(x.dtype), x * odd.astype(x.dtype)], axis=0)


def own_lanes(stacked, group_size):
    pairs = LANES // (2 * group_size)
    rows = stacked.shape[0] // pairs
    pair_of = lane_group((rows, LANES), 2 * group_size)
    out = stacked[:rows]
    for pair in range(1, pairs):
        out = jnp.where(pair_of == pair, stacked[pair * rows : (pair + 1) * rows], out)
    return out


def matmul(a, b):
    return jnp.dot(a, b, preferred_element_type=F32)


def pair_product(x, table, group_size):
    out = matmul(x, table)
    tok = out.shape[1] // 2
    return jnp.concatenate([out[:group_size, :tok], out[group_size:, tok:]], axis=0)


def turned(row, size):
    ring = pltpu.roll(jnp.broadcast_to(row, (size, size)), 0, 1, stride=1, stride_axis=0)
    return ring.astype(BF16)


def series(x):
    out = jnp.ones_like(x)
    for n in range(TERMS, 1, -1):
        out = 1.0 - x / n * out
    return out


def tile_of(i):
    return pl.ds(pl.multiple_of(i * LANES, LANES), LANES)


def spans(channels):
    size = max(2 * LANES, channels // PARTS)
    return [pl.ds(start, size) for start in range(0, channels, size)]


def gated(k, v, out_ref):
    for start in range(0, out_ref.shape[0], LANES):
        at = pl.ds(start, LANES)
        out_ref[at, :] = (k[:, at].astype(F32) * v[:, at].astype(F32)).astype(BF16).T


def first_kernel(k_hbm, v_hbm, out_ref, *refs):
    later, (k_ref, v_ref, sems) = refs[:-3], refs[-3:]
    chunk = out_ref.shape[0]
    copies = []
    for n, to in enumerate((k_ref, v_ref) + later):
        source = (k_hbm, v_hbm)[n % 2].at[:, pl.ds(0, chunk) if n < 2 else pl.ds(chunk, to.shape[1])]
        copies.append(pltpu.make_async_copy(source, to, sems.at[n]))
        copies[-1].start()
    copies[0].wait()
    copies[1].wait()
    gated(k_ref, v_ref, out_ref)
    for copy in copies[2:]:
        copy.wait()


def prep_kernel(
    group_size, bits, place_ref, u_refs, gain_hbm, taps_hbm, rate_hbm, residue_hbm, resid_hbm, q_hbm, k_hbm,
    base_ref, gate_ref, key_ref, upper_ref, square_ref, leave_ref, entry_ref, factor_ref, keep_ref, take_ref,
    taps, impulse, rates, weights, lower_ref,
    gain_ref, taps_ref, rate_ref, residue_ref, resid_ref, q_ref, k_ref, sems,
):
    tok = u_refs[0].shape[1]
    channels = sum(ref.shape[0] for ref in u_refs)
    poles, groups = rate_ref.shape
    per, width = LANES // group_size, 2 * group_size
    sources = (taps_hbm, rate_hbm, residue_hbm, gain_hbm, resid_hbm, q_hbm, k_hbm)
    places = (taps_ref, rate_ref, residue_ref, gain_ref, resid_ref, q_ref, k_ref)
    copies = [pltpu.make_async_copy(a, b, sems.at[n]) for n, (a, b) in enumerate(zip(sources, places))]
    for copy in copies:
        copy.start()
    row = lax.broadcasted_iota(jnp.int32, (tok, tok), 0)
    col = lax.broadcasted_iota(jnp.int32, (tok, tok), 1)
    causal = jnp.where(row <= col, 1.0, 0.0).astype(BF16)
    live = jnp.where(place_ref[0] > 0, 1.0, 0.0)
    future = jnp.where(row <= col, 0.0, live).astype(BF16)

    copies[0].wait()
    taps[...] = taps_ref[...].astype(F32)

    def taps_tables(i, _):
        for k in range(SPAN):
            ring = turned(taps[pl.ds(i * SPAN + k, 1), :], tok)
            at, cols = i * (SPAN // 2) + k // 2, pl.ds(k % 2 * tok, tok)
            lower_ref[at, :, cols] = ring * causal
            upper_ref[at, :, cols] = ring * future
        return 0

    lax.fori_loop(0, groups // SPAN, taps_tables, 0)

    copies[1].wait()
    copies[2].wait()
    twice = 2.0 * rate_ref[...]
    weight = residue_ref[...] * jnp.sqrt(jnp.where(twice < SMALL, twice * series(twice), 1.0 - jnp.exp(-twice)))
    for g in range(groups):
        at = pl.ds(g * poles, poles)
        rates[at, :] = jnp.broadcast_to(rate_ref[:, g : g + 1], (poles, tok))
        weights[at, :] = jnp.broadcast_to(weight[:, g : g + 1], (poles, tok))

    position = lax.broadcasted_iota(jnp.int32, (poles, tok), 1)
    now = position.astype(F32)
    ahead = (position + 1).astype(F32)
    remain = (tok - 1 - position).astype(F32)
    place = place_ref[0]
    lane_of = lane_group((poles, LANES), group_size)

    def decays(i, _):
        spread = jnp.zeros((poles, LANES), F32)
        for k in range(per):
            at = pl.ds(pl.multiple_of((i * per + k) * poles, poles), poles)
            rate, weight = rates[at, :], weights[at, :]
            impulse[pl.ds(i * per + k, 1), :] = jnp.sum(weight * jnp.exp(-rate * now), axis=0, keepdims=True)
            leave_ref[i, pl.ds(k // 2 * poles, poles), pl.ds(k % 2 * tok, tok)] = jnp.exp(-rate * remain)
            weights[at, :] = weight * jnp.exp(-rate * ahead)
            spread = jnp.where(lane_of == k, rate, spread)
        spread = spread * tok
        at = tile_of(i)
        for step, bit in enumerate(bits):
            late = (place & bit) != 0
            behind = (place & (bit - 1)).astype(F32)
            whole = jnp.exp(-spread * bit)
            factor_ref[step, :, at] = jnp.where(late, jnp.exp(-spread * behind), 0.0)
            keep_ref[step, :, at] = jnp.where(late, 1.0, whole)
            take_ref[step, :, at] = jnp.where(late, whole, 1.0)
        return 0

    lax.fori_loop(0, channels // LANES, decays, 0, unroll=2)

    def square_tables(i, _):
        for k in range(SPAN):
            ring = turned(impulse[pl.ds(i * SPAN + k, 1), :], tok)
            square_ref[i * (SPAN // 2) + k // 2, :, pl.ds(k % 2 * tok, tok)] = ring * causal
        return 0

    lax.fori_loop(0, groups // SPAN, square_tables, 0)

    for pair in range(channels // width):
        at = pl.ds(pair * width, width)
        base_ref[at, :] = pair_product(rows_of(u_refs, pair * width, width), lower_ref[pair], group_size)

    for copy in copies[3:]:
        copy.wait()
    for i in range(channels // LANES):
        at = pl.ds(i * LANES, LANES)
        gate = q_ref[:, at].T.astype(F32)
        gate_ref[at, :] = gate
        base_ref[at, :] = resid_ref[:, at].T.astype(F32) + gate * base_ref[at, :]
        key_ref[at, :] = (k_ref[:, at].astype(F32) * gain_ref[i : i + 1, :].astype(F32)).T
        enter = weights[pl.ds(i * per * poles, per * poles), :]
        entry_ref[i // 2, :, pl.ds(i % 2 * per * poles, per * poles)] = enter.T.astype(BF16)


def mix_kernel(group_size, first, halo_ref, upper_ref, base_ref, gate_ref, key_ref, *refs):
    before, (mixed_ref, z_ref, sum_ref) = refs[:-3], refs[-3:]
    channels, tok = halo_ref.shape
    width = 2 * group_size
    total = jnp.zeros((width, tok), F32)
    for pair in range(channels // width):
        at, there = pl.ds(pair * width, width), pl.ds(first + pair * width, width)
        past = pair_product(halo_ref[at, :], upper_ref[first // width + pair], group_size)
        mixed = (base_ref[there, :] + gate_ref[there, :] * past).astype(BF16)
        mixed_ref[at, :] = mixed
        mixed = mixed.astype(F32)
        z_ref[at, :] = key_ref[there, :] * mixed
        total = total + mixed * mixed
    total = jnp.sum(total, axis=0, keepdims=True)
    for ref in before:
        total = total + ref[...]
    sum_ref[...] = total


def rows_of(refs, start, size):
    for ref in refs:
        if start < ref.shape[0]:
            return ref[pl.ds(start, size), :]
        start -= ref.shape[0]


def turn_kernel(group_size, z_refs, zb_ref):
    for i in range(zb_ref.shape[0]):
        zb_ref[i] = by_parity(rows_of(z_refs, i * LANES, LANES).astype(BF16).T, group_size)


def written(tile, width, out_hbm, out_ref, sem):
    copies = []
    for n, part in enumerate(spans(out_ref.shape[1])):
        for start in range(part.start, part.start + part.size, width):
            out_ref[:, pl.ds(start, width)] = tile(start // width)
        copies.append(pltpu.make_async_copy(out_ref.at[:, part], out_hbm.at[:, part], sem.at[n]))
        copies[-1].start()
    for copy in copies:
        copy.wait()


def out_kernel(mixed_refs, out_hbm, out_ref, sem):
    written(lambda i: rows_of(mixed_refs, i * LANES, LANES).T, LANES, out_hbm, out_ref, sem)


def state_kernel(group_size, width, parts, *refs):
    sums, (leave_ref, zb_ref, state_ref, sent_ref, scale_ref) = refs[:parts], refs[parts:]
    square_sum = sums[0][...]
    for other in sums[1:]:
        square_sum = square_sum + other[...]
    scale = lax.rsqrt(square_sum / width + 1e-06)
    scale_ref[...] = scale
    twice = jnp.concatenate([scale, scale], axis=1)
    for i in range(leave_ref.shape[0]):
        at = pl.ds(i * LANES, LANES)
        leaving = (leave_ref[i] * twice).astype(BF16)
        state = own_lanes(matmul(leaving, zb_ref[i]), group_size)
        state_ref[:, at] = state
        sent_ref[:, at] = state.astype(BF16)


def local_kernel(group_size, scale_ref, z_refs, square_ref, local_ref):
    width = 2 * group_size
    scale = scale_ref[...]
    first = 0
    for z_ref in z_refs:

        def body(i, _, z_ref=z_ref, first=first):
            rows = []
            for pair in range(LANES // width):
                at = pl.ds(pl.multiple_of(i * LANES + pair * width, width), width)
                y = (z_ref[at, :] * scale).astype(BF16)
                table = square_ref[(first + i * LANES) // width + pair]
                rows.append(pair_product(y, table, group_size))
            local_ref[:, tile_of(first // LANES + i)] = jnp.concatenate(rows, axis=0).T
            return 0

        lax.fori_loop(0, z_ref.shape[0] // LANES, body, 0, unroll=4)
        first += z_ref.shape[0]


def final_kernel(group_size, rounds, *refs):
    got, (factor_ref, entry_ref, local_ref, q_ref, out_hbm, out_ref, sem) = refs[:rounds], refs[rounds:]
    poles, _ = got[0].shape
    per = LANES // group_size
    group_of = lane_group((poles, LANES), group_size)
    empty = jnp.zeros((per * poles, LANES), BF16)

    def spread(i):
        at = pl.ds(i * LANES, LANES)
        carried = factor_ref[0, :, at] * got[0][:, at].astype(F32)
        for step in range(1, rounds):
            carried = carried + factor_ref[step, :, at] * got[step][:, at].astype(F32)
        return jnp.concatenate([jnp.where(group_of == g, carried, 0.0) for g in range(per)], axis=0).astype(BF16)

    def tile(i):
        at = pl.ds(2 * i * LANES, 2 * LANES)
        left = jnp.concatenate([spread(2 * i), empty], axis=1)
        right = jnp.concatenate([empty, spread(2 * i + 1)], axis=1)
        conv = local_ref[:, at] + matmul(entry_ref[i], jnp.concatenate([left, right], axis=0))
        return (q_ref[:, at].astype(F32) * conv).astype(BF16)

    written(tile, 2 * LANES, out_hbm, out_ref, sem)


def held(shape, dtype):
    return jax.ShapeDtypeStruct(shape, dtype)


def call(kernel, outs, scratch, flops, *args, **more):
    places = more.get("in_specs", [VMEM] * len(args))
    args = [pltpu.with_memory_space_constraint(a, pltpu.HBM) if s is HBM else a for a, s in zip(args, places)]
    specs = [[s] * len(a) if isinstance(a, list) else s for a, s in zip(args, places)]
    size = sum(a.size * a.dtype.itemsize for a in jax.tree.leaves(args))
    return pl.pallas_call(
        kernel,
        in_specs=specs,
        out_specs=more.get("out_specs", jax.tree.map(lambda _: VMEM, outs)),
        out_shape=outs,
        scratch_shapes=scratch,
        cost_estimate=pl.CostEstimate(flops=flops, bytes_accessed=size, transcendentals=0),
        compiler_params=pltpu.CompilerParams(vmem_limit_bytes=GRANT),
    )(*args)


def per_device(resid, q_mr, k_mr, v_mr, mr_taps, norm_gain, q_lr, k_lr, pole_rate, residue):
    tok, channels = resid.shape
    groups, tap_count = mr_taps.shape
    poles = pole_rate.shape[0]
    group_size = channels // groups
    assert tap_count == tok and channels % (16 * LANES) == 0 and LANES % (2 * group_size) == 0
    tiles, per = channels // LANES, LANES // group_size
    shards = lax.axis_size("ctx")
    bits = [1 << b for b in range((shards - 1).bit_length())]
    rounds = len(bits)
    place = lax.axis_index("ctx").astype(jnp.int32).reshape(1)
    work = 4 * tok * tok * channels

    sizes = [channels * FIRST // 16, channels - channels * FIRST // 16]
    firsts = [0, sizes[0]]
    rows = pltpu.VMEM((tok, channels), BF16)
    part = pltpu.VMEM((tok, sizes[0]), BF16)
    sem = pltpu.SemaphoreType.DMA((PARTS,))
    u0, k1, v1 = call(
        first_kernel, [held((sizes[0], tok), BF16)] + [held((tok, sizes[1]), BF16)] * 2,
        [part, part, pltpu.SemaphoreType.DMA((4,))], work // 8, k_mr, v_mr, in_specs=[HBM, HBM],
    )
    halo = [passed_on(u0, True)]
    u = [u0, call(gated, held((sizes[1], tok), BF16), [], work // 8, k1, v1)]
    halo.append(passed_on(u[1], False))

    tall = held((channels, tok), F32)
    table = held((groups // 2, tok, 2 * tok), BF16)
    steps = held((rounds, poles, channels), F32)
    base, gate, key, upper, square, leave, entry, factor, keep, take = call(
        functools.partial(prep_kernel, group_size, bits),
        (
            tall, tall, tall, table, table,
            held((tiles, per // 2 * poles, 2 * tok), F32),
            held((tiles // 2, tok, 2 * per * poles), BF16),
            steps, steps, steps,
        ),
        [
            pltpu.VMEM((groups, tok), F32), pltpu.VMEM((groups, tok), F32), pltpu.VMEM((groups * poles, tok), F32),
            pltpu.VMEM((groups * poles, tok), F32), pltpu.VMEM(table.shape, BF16), pltpu.VMEM((tiles, LANES), BF16),
            pltpu.VMEM((groups, tok), BF16), pltpu.VMEM((poles, groups), F32), pltpu.VMEM((poles, groups), F32),
            rows, rows, rows, pltpu.SemaphoreType.DMA((7,)),
        ],
        8 * work,
        place, u, norm_gain.reshape(tiles, LANES), mr_taps, pole_rate, residue, resid, q_mr, k_lr,
        in_specs=[SMEM, VMEM] + [HBM] * 7,
    )
    mixed_t, z, square_sum = [], [], []
    for first, past in zip(firsts, halo):
        outs = call(
            functools.partial(mix_kernel, group_size, first),
            (held(past.shape, BF16), held(past.shape, F32), held((1, tok), F32)),
            [],
            work // 2,
            past, upper, base, gate, key, *square_sum,
        )
        mixed_t.append(outs[0])
        z.append(outs[1])
        square_sum = [outs[2]]
    square_sum = square_sum[0]
    sums = everyone(square_sum, "tp")
    zb = call(
        functools.partial(turn_kernel, group_size), held((tiles, 2 * tok, LANES), BF16), [], work // 2, z
    )
    small = (poles, channels)
    state, sent, scale = call(
        functools.partial(state_kernel, group_size, channels * lax.axis_size("tp"), len(sums)),
        (held(small, F32), held(small, BF16), held((1, tok), F32)),
        [],
        work // 8,
        *sums, leave, zb,
    )
    local = call(
        functools.partial(local_kernel, group_size),
        held((tok, channels), F32),
        [],
        work,
        scale, z, square,
    )
    got = []
    for step, bit in enumerate(bits):
        got.append(swapped(sent, "ctx", bit))
        state = keep[step] * state + take[step] * got[step].astype(F32)
        sent = state.astype(BF16)
    mixed = call(out_kernel, held((tok, channels), BF16), [rows, sem], work // 4, mixed_t, out_specs=HBM)
    lr_out = call(
        functools.partial(final_kernel, group_size, rounds),
        held((tok, channels), BF16),
        [rows, sem],
        work // 8,
        *got, factor, entry, local, q_lr,
        out_specs=HBM,
    )
    return (mixed, lr_out)


def solution(mesh):
    whole, tables = P("ctx", "tp"), P(None, "tp")
    placed = (whole,) * 4 + (P("tp", None), P("tp")) + (whole,) * 2 + (tables,) * 2
    return jax.shard_map(per_device, mesh=mesh, in_specs=placed, out_specs=(whole, whole), check_vma=False)
```

```python
import functools

import jax
import jax.numpy as jnp
from jax import lax
from jax.experimental import pallas as pl
from jax.experimental.pallas import tpu as pltpu
from jax.sharding import PartitionSpec as P


LANES = 128
GRANT = 16 << 20
F32, BF16 = jnp.float32, jnp.bfloat16
VMEM = pl.BlockSpec(memory_space=pltpu.VMEM)
SMEM = pl.BlockSpec(memory_space=pltpu.SMEM)
HBM = pl.BlockSpec(memory_space=pltpu.HBM)
PARTS = 4
FIRST = 8
SMALL, TERMS = 0.5, 10
SPAN = 16


def passed_on(x, close):
    shards = lax.axis_size("ctx")
    pairs = [(i, (i + 1) % shards) for i in range(shards if close else shards - 1)]
    return lax.ppermute(x, "ctx", pairs)


def swapped(x, axis, bit):
    peers = lax.axis_size(axis)
    return lax.ppermute(x, axis, [(i, i ^ bit) for i in range(peers) if i ^ bit < peers])


def everyone(x, axis):
    peers = lax.axis_size(axis)
    if peers & (peers - 1) == 0:
        return [x] + [swapped(x, axis, bit) for bit in range(1, peers)]
    turns = [[(i, (i + by) % peers) for i in range(peers)] for by in range(1, peers)]
    return [x] + [lax.ppermute(x, axis, turn) for turn in turns]


def lane_group(shape, width):
    return lax.broadcasted_iota(jnp.int32, shape, 1) // width


def by_parity(x, group_size):
    odd = jnp.where(lane_group((1, LANES), group_size) % 2 == 1, 1.0, 0.0)
    return jnp.concatenate([x * (1.0 - odd).astype(x.dtype), x * odd.astype(x.dtype)], axis=0)


def own_lanes(stacked, group_size):
    pairs = LANES // (2 * group_size)
    rows = stacked.shape[0] // pairs
    pair_of = lane_group((rows, LANES), 2 * group_size)
    out = stacked[:rows]
    for pair in range(1, pairs):
        out = jnp.where(pair_of == pair, stacked[pair * rows : (pair + 1) * rows], out)
    return out


def matmul(a, b):
    return jnp.dot(a, b, preferred_element_type=F32)


def own_half(out, group_size):
    tok = out.shape[1] // 2
    return jnp.concatenate([out[:group_size, :tok], out[group_size:, tok:]], axis=0)


def pair_product(x, table, group_size):
    return own_half(matmul(x, table), group_size)


def turned(row, size):
    ring = pltpu.roll(jnp.broadcast_to(row, (size, size)), 0, 1, stride=1, stride_axis=0)
    return ring.astype(BF16)


def series(x):
    out = jnp.ones_like(x)
    for n in range(TERMS, 1, -1):
        out = 1.0 - x / n * out
    return out


def tile_of(i):
    return pl.ds(pl.multiple_of(i * LANES, LANES), LANES)


def spans(channels):
    size = max(2 * LANES, channels // PARTS)
    return [pl.ds(start, size) for start in range(0, channels, size)]


def gated(k, v, out_ref):
    for start in range(0, out_ref.shape[0], LANES):
        at = pl.ds(start, LANES)
        out_ref[at, :] = (k[:, at].astype(F32) * v[:, at].astype(F32)).astype(BF16).T


def first_kernel(k_hbm, v_hbm, out_ref, *refs):
    later, (k_ref, v_ref, sems) = refs[:-3], refs[-3:]
    chunk = out_ref.shape[0]
    copies = []
    for n, to in enumerate((k_ref, v_ref) + later):
        source = (k_hbm, v_hbm)[n % 2].at[:, pl.ds(0, chunk) if n < 2 else pl.ds(chunk, to.shape[1])]
        copies.append(pltpu.make_async_copy(source, to, sems.at[n]))
        copies[-1].start()
    copies[0].wait()
    copies[1].wait()
    gated(k_ref, v_ref, out_ref)
    for copy in copies[2:]:
        copy.wait()


def prep_kernel(
    group_size, bits, place_ref, u_refs, gain_hbm, taps_hbm, rate_hbm, residue_hbm, resid_hbm, q_hbm, k_hbm,
    base_ref, gate_ref, key_ref, upper_ref, impulse, leave_ref, entry_ref, factor_ref, keep_ref, take_ref,
    taps, rates, weights, lower_ref,
    gain_ref, taps_ref, rate_ref, residue_ref, resid_ref, q_ref, k_ref, sems,
):
    tok = u_refs[0].shape[1]
    channels = sum(ref.shape[0] for ref in u_refs)
    poles, groups = rate_ref.shape
    per, width = LANES // group_size, 2 * group_size
    sources = (taps_hbm, rate_hbm, residue_hbm, gain_hbm, resid_hbm, q_hbm, k_hbm)
    places = (taps_ref, rate_ref, residue_ref, gain_ref, resid_ref, q_ref, k_ref)
    copies = [pltpu.make_async_copy(a, b, sems.at[n]) for n, (a, b) in enumerate(zip(sources, places))]
    for copy in copies:
        copy.start()
    row = lax.broadcasted_iota(jnp.int32, (tok, tok), 0)
    col = lax.broadcasted_iota(jnp.int32, (tok, tok), 1)
    causal = jnp.where(row <= col, 1.0, 0.0).astype(BF16)
    live = jnp.where(place_ref[0] > 0, 1.0, 0.0)
    future = jnp.where(row <= col, 0.0, live).astype(BF16)

    copies[0].wait()
    taps[...] = taps_ref[...].astype(F32)

    def taps_tables(i, _):
        for k in range(SPAN):
            ring = turned(taps[pl.ds(i * SPAN + k, 1), :], tok)
            at, cols = i * (SPAN // 2) + k // 2, pl.ds(k % 2 * tok, tok)
            lower_ref[at, :, cols] = ring * causal
            upper_ref[at, :, cols] = ring * future
        return 0

    lax.fori_loop(0, groups // SPAN, taps_tables, 0)

    copies[1].wait()
    copies[2].wait()
    twice = 2.0 * rate_ref[...]
    weight = residue_ref[...] * jnp.sqrt(jnp.where(twice < SMALL, twice * series(twice), 1.0 - jnp.exp(-twice)))
    for g in range(groups):
        at = pl.ds(g * poles, poles)
        rates[at, :] = jnp.broadcast_to(rate_ref[:, g : g + 1], (poles, tok))
        weights[at, :] = jnp.broadcast_to(weight[:, g : g + 1], (poles, tok))

    position = lax.broadcasted_iota(jnp.int32, (poles, tok), 1)
    now = position.astype(F32)
    ahead = (position + 1).astype(F32)
    remain = (tok - 1 - position).astype(F32)
    place = place_ref[0]
    lane_of = lane_group((poles, LANES), group_size)

    def decays(i, _):
        spread = jnp.zeros((poles, LANES), F32)
        for k in range(per):
            at = pl.ds(pl.multiple_of((i * per + k) * poles, poles), poles)
            rate, weight = rates[at, :], weights[at, :]
            impulse[pl.ds(i * per + k, 1), :] = jnp.sum(weight * jnp.exp(-rate * now), axis=0, keepdims=True)
            leave_ref[i, pl.ds(k // 2 * poles, poles), pl.ds(k % 2 * tok, tok)] = jnp.exp(-rate * remain)
            weights[at, :] = weight * jnp.exp(-rate * ahead)
            spread = jnp.where(lane_of == k, rate, spread)
        spread = spread * tok
        at = tile_of(i)
        for step, bit in enumerate(bits):
            late = (place & bit) != 0
            behind = (place & (bit - 1)).astype(F32)
            whole = jnp.exp(-spread * bit)
            factor_ref[step, :, at] = jnp.where(late, jnp.exp(-spread * behind), 0.0)
            keep_ref[step, :, at] = jnp.where(late, 1.0, whole)
            take_ref[step, :, at] = jnp.where(late, whole, 1.0)
        return 0

    lax.fori_loop(0, channels // LANES, decays, 0, unroll=2)

    for pair in range(channels // width):
        at = pl.ds(pair * width, width)
        base_ref[at, :] = pair_product(rows_of(u_refs, pair * width, width), lower_ref[pair], group_size)

    for copy in copies[3:]:
        copy.wait()
    for i in range(channels // LANES):
        at = pl.ds(i * LANES, LANES)
        gate = q_ref[:, at].T.astype(F32)
        gate_ref[at, :] = gate
        base_ref[at, :] = resid_ref[:, at].T.astype(F32) + gate * base_ref[at, :]
        key_ref[at, :] = (k_ref[:, at].astype(F32) * gain_ref[i : i + 1, :].astype(F32)).T
        enter = weights[pl.ds(i * per * poles, per * poles), :]
        entry_ref[i // 2, :, pl.ds(i % 2 * per * poles, per * poles)] = enter.T.astype(BF16)


def square_kernel(impulse_ref, square_ref):
    groups, tok = impulse_ref.shape
    row = lax.broadcasted_iota(jnp.int32, (tok, tok), 0)
    col = lax.broadcasted_iota(jnp.int32, (tok, tok), 1)
    causal = jnp.where(row <= col, 1.0, 0.0).astype(BF16)

    def body(i, _):
        for k in range(SPAN):
            ring = turned(impulse_ref[pl.ds(i * SPAN + k, 1), :], tok)
            square_ref[i * (SPAN // 2) + k // 2, :, pl.ds(k % 2 * tok, tok)] = ring * causal
        return 0

    lax.fori_loop(0, groups // SPAN, body, 0)


def mix_kernel(group_size, first, halo_ref, upper_ref, base_ref, gate_ref, key_ref, *refs):
    before, (mixed_ref, z_ref, sum_ref) = refs[:-3], refs[-3:]
    channels, tok = halo_ref.shape
    width = 2 * group_size
    total = jnp.zeros((width, tok), F32)
    for pair in range(channels // width):
        at, there = pl.ds(pair * width, width), pl.ds(first + pair * width, width)
        past = pair_product(halo_ref[at, :], upper_ref[first // width + pair], group_size)
        mixed = (base_ref[there, :] + gate_ref[there, :] * past).astype(BF16)
        mixed_ref[at, :] = mixed
        mixed = mixed.astype(F32)
        z_ref[at, :] = key_ref[there, :] * mixed
        total = total + mixed * mixed
    total = jnp.sum(total, axis=0, keepdims=True)
    for ref in before:
        total = total + ref[...]
    sum_ref[...] = total


def rows_of(refs, start, size):
    for ref in refs:
        if start < ref.shape[0]:
            return ref[pl.ds(start, size), :]
        start -= ref.shape[0]


def turn_kernel(group_size, z_refs, zb_ref):
    for i in range(zb_ref.shape[0]):
        zb_ref[i] = by_parity(rows_of(z_refs, i * LANES, LANES).astype(BF16).T, group_size)


def written(tile, width, out_hbm, out_ref, sem):
    copies = []
    for n, part in enumerate(spans(out_ref.shape[1])):
        for start in range(part.start, part.start + part.size, width):
            out_ref[:, pl.ds(start, width)] = tile(start // width)
        copies.append(pltpu.make_async_copy(out_ref.at[:, part], out_hbm.at[:, part], sem.at[n]))
        copies[-1].start()
    for copy in copies:
        copy.wait()


def out_kernel(mixed_refs, out_hbm, out_ref, sem):
    written(lambda i: rows_of(mixed_refs, i * LANES, LANES).T, LANES, out_hbm, out_ref, sem)


def state_kernel(group_size, width, parts, *refs):
    sums, (leave_ref, zb_ref, state_ref, sent_ref, scale_ref) = refs[:parts], refs[parts:]
    square_sum = sums[0][...]
    for other in sums[1:]:
        square_sum = square_sum + other[...]
    scale = lax.rsqrt(square_sum / width + 1e-06)
    scale_ref[...] = scale
    twice = jnp.concatenate([scale, scale], axis=1)
    for i in range(leave_ref.shape[0]):
        at = pl.ds(i * LANES, LANES)
        leaving = (leave_ref[i] * twice).astype(BF16)
        state = own_lanes(matmul(leaving, zb_ref[i]), group_size)
        state_ref[:, at] = state
        sent_ref[:, at] = state.astype(BF16)


def local_kernel(group_size, scale_ref, z_refs, square_ref, local_ref):
    width = 2 * group_size
    scale = scale_ref[...]
    first = 0
    for z_ref in z_refs:

        def body(i, _, z_ref=z_ref, first=first):
            rows = []
            for pair in range(LANES // width):
                at = pl.ds(pl.multiple_of(i * LANES + pair * width, width), width)
                y = z_ref[at, :] * scale
                high = y.astype(BF16)
                low = (y - high.astype(F32)).astype(BF16)
                table = square_ref[(first + i * LANES) // width + pair]
                out = matmul(jnp.concatenate([high, low], axis=0), table)
                rows.append(own_half(out[:width] + out[width:], group_size))
            local_ref[:, tile_of(first // LANES + i)] = jnp.concatenate(rows, axis=0).T
            return 0

        lax.fori_loop(0, z_ref.shape[0] // LANES, body, 0, unroll=4)
        first += z_ref.shape[0]


def final_kernel(group_size, rounds, *refs):
    got, (factor_ref, entry_ref, local_ref, q_ref, out_hbm, out_ref, sem) = refs[:rounds], refs[rounds:]
    poles, _ = got[0].shape
    per = LANES // group_size
    group_of = lane_group((poles, LANES), group_size)
    empty = jnp.zeros((per * poles, LANES), BF16)

    def spread(i):
        at = pl.ds(i * LANES, LANES)
        carried = factor_ref[0, :, at] * got[0][:, at].astype(F32)
        for step in range(1, rounds):
            carried = carried + factor_ref[step, :, at] * got[step][:, at].astype(F32)
        return jnp.concatenate([jnp.where(group_of == g, carried, 0.0) for g in range(per)], axis=0).astype(BF16)

    def tile(i):
        at = pl.ds(2 * i * LANES, 2 * LANES)
        left = jnp.concatenate([spread(2 * i), empty], axis=1)
        right = jnp.concatenate([empty, spread(2 * i + 1)], axis=1)
        conv = local_ref[:, at] + matmul(entry_ref[i], jnp.concatenate([left, right], axis=0))
        return (q_ref[:, at].astype(F32) * conv).astype(BF16)

    written(tile, 2 * LANES, out_hbm, out_ref, sem)


def held(shape, dtype):
    return jax.ShapeDtypeStruct(shape, dtype)


def call(kernel, outs, scratch, flops, *args, **more):
    places = more.get("in_specs", [VMEM] * len(args))
    args = [pltpu.with_memory_space_constraint(a, pltpu.HBM) if s is HBM else a for a, s in zip(args, places)]
    specs = [[s] * len(a) if isinstance(a, list) else s for a, s in zip(args, places)]
    size = sum(a.size * a.dtype.itemsize for a in jax.tree.leaves(args))
    return pl.pallas_call(
        kernel,
        in_specs=specs,
        out_specs=more.get("out_specs", jax.tree.map(lambda _: VMEM, outs)),
        out_shape=outs,
        scratch_shapes=scratch,
        cost_estimate=pl.CostEstimate(flops=flops, bytes_accessed=size, transcendentals=0),
        compiler_params=pltpu.CompilerParams(vmem_limit_bytes=GRANT),
    )(*args)


def per_device(resid, q_mr, k_mr, v_mr, mr_taps, norm_gain, q_lr, k_lr, pole_rate, residue):
    tok, channels = resid.shape
    groups, tap_count = mr_taps.shape
    poles = pole_rate.shape[0]
    group_size = channels // groups
    assert tap_count == tok and channels % (16 * LANES) == 0 and LANES % (2 * group_size) == 0
    tiles, per = channels // LANES, LANES // group_size
    shards = lax.axis_size("ctx")
    bits = [1 << b for b in range((shards - 1).bit_length())]
    rounds = len(bits)
    place = lax.axis_index("ctx").astype(jnp.int32).reshape(1)
    work = 4 * tok * tok * channels

    sizes = [channels * FIRST // 16, channels - channels * FIRST // 16]
    firsts = [0, sizes[0]]
    rows = pltpu.VMEM((tok, channels), BF16)
    part = pltpu.VMEM((tok, sizes[0]), BF16)
    sem = pltpu.SemaphoreType.DMA((PARTS,))
    u0, k1, v1 = call(
        first_kernel, [held((sizes[0], tok), BF16)] + [held((tok, sizes[1]), BF16)] * 2,
        [part, part, pltpu.SemaphoreType.DMA((4,))], work // 8, k_mr, v_mr, in_specs=[HBM, HBM],
    )
    halo = [passed_on(u0, True)]
    u = [u0, call(gated, held((sizes[1], tok), BF16), [], work // 8, k1, v1)]
    halo.append(passed_on(u[1], False))

    tall = held((channels, tok), F32)
    table = held((groups // 2, tok, 2 * tok), BF16)
    steps = held((rounds, poles, channels), F32)
    base, gate, key, upper, impulse, leave, entry, factor, keep, take = call(
        functools.partial(prep_kernel, group_size, bits),
        (
            tall, tall, tall, table, held((groups, tok), F32),
            held((tiles, per // 2 * poles, 2 * tok), F32),
            held((tiles // 2, tok, 2 * per * poles), BF16),
            steps, steps, steps,
        ),
        [
            pltpu.VMEM((groups, tok), F32), pltpu.VMEM((groups * poles, tok), F32),
            pltpu.VMEM((groups * poles, tok), F32), pltpu.VMEM(table.shape, BF16), pltpu.VMEM((tiles, LANES), BF16),
            pltpu.VMEM((groups, tok), BF16), pltpu.VMEM((poles, groups), F32), pltpu.VMEM((poles, groups), F32),
            rows, rows, rows, pltpu.SemaphoreType.DMA((7,)),
        ],
        8 * work,
        place, u, norm_gain.reshape(tiles, LANES), mr_taps, pole_rate, residue, resid, q_mr, k_lr,
        in_specs=[SMEM, VMEM] + [HBM] * 7,
    )
    mixed_t, z, square_sum = [], [], []
    for first, past in zip(firsts, halo):
        outs = call(
            functools.partial(mix_kernel, group_size, first),
            (held(past.shape, BF16), held(past.shape, F32), held((1, tok), F32)),
            [],
            work // 2,
            past, upper, base, gate, key, *square_sum,
        )
        mixed_t.append(outs[0])
        z.append(outs[1])
        square_sum = [outs[2]]
    square_sum = square_sum[0]
    sums = everyone(square_sum, "tp")
    zb = call(
        functools.partial(turn_kernel, group_size), held((tiles, 2 * tok, LANES), BF16), [], work // 2, z
    )
    small = (poles, channels)
    state, sent, scale = call(
        functools.partial(state_kernel, group_size, channels * lax.axis_size("tp"), len(sums)),
        (held(small, F32), held(small, BF16), held((1, tok), F32)),
        [],
        work // 8,
        *sums, leave, zb,
    )
    square = call(square_kernel, table, [], work, impulse)
    local = call(
        functools.partial(local_kernel, group_size),
        held((tok, channels), F32),
        [],
        work,
        scale, z, square,
    )
    got = []
    for step, bit in enumerate(bits):
        got.append(swapped(sent, "ctx", bit))
        state = keep[step] * state + take[step] * got[step].astype(F32)
        sent = state.astype(BF16)
    mixed = call(out_kernel, held((tok, channels), BF16), [rows, sem], work // 4, mixed_t, out_specs=HBM)
    lr_out = call(
        functools.partial(final_kernel, group_size, rounds),
        held((tok, channels), BF16),
        [rows, sem],
        work // 8,
        *got, factor, entry, local, q_lr,
        out_specs=HBM,
    )
    return (mixed, lr_out)


def solution(mesh):
    whole, tables = P("ctx", "tp"), P(None, "tp")
    placed = (whole,) * 4 + (P("tp", None), P("tp")) + (whole,) * 2 + (tables,) * 2
    return jax.shard_map(per_device, mesh=mesh, in_specs=placed, out_specs=(whole, whole), check_vma=False)
```

```python
import functools

import jax
import jax.numpy as jnp
from jax import lax
from jax.experimental import pallas as pl
from jax.experimental.pallas import tpu as pltpu
from jax.sharding import PartitionSpec as P


LANES = 128
GRANT = 16 << 20
F32, BF16 = jnp.float32, jnp.bfloat16
VMEM = pl.BlockSpec(memory_space=pltpu.VMEM)
SMEM = pl.BlockSpec(memory_space=pltpu.SMEM)
HBM = pl.BlockSpec(memory_space=pltpu.HBM)
PARTS = 4
FIRST = 10
SMALL, TERMS = 0.5, 10
SPAN = 16


def passed_on(x, close):
    shards = lax.axis_size("ctx")
    pairs = [(i, (i + 1) % shards) for i in range(shards if close else shards - 1)]
    return lax.ppermute(x, "ctx", pairs)


def swapped(x, axis, bit):
    peers = lax.axis_size(axis)
    return lax.ppermute(x, axis, [(i, i ^ bit) for i in range(peers) if i ^ bit < peers])


def everyone(x, axis):
    peers = lax.axis_size(axis)
    if peers & (peers - 1) == 0:
        return [x] + [swapped(x, axis, bit) for bit in range(1, peers)]
    turns = [[(i, (i + by) % peers) for i in range(peers)] for by in range(1, peers)]
    return [x] + [lax.ppermute(x, axis, turn) for turn in turns]


def lane_group(shape, width):
    return lax.broadcasted_iota(jnp.int32, shape, 1) // width


def by_parity(x, group_size):
    odd = jnp.where(lane_group((1, LANES), group_size) % 2 == 1, 1.0, 0.0)
    return jnp.concatenate([x * (1.0 - odd).astype(x.dtype), x * odd.astype(x.dtype)], axis=0)


def own_lanes(stacked, group_size):
    pairs = LANES // (2 * group_size)
    rows = stacked.shape[0] // pairs
    pair_of = lane_group((rows, LANES), 2 * group_size)
    out = stacked[:rows]
    for pair in range(1, pairs):
        out = jnp.where(pair_of == pair, stacked[pair * rows : (pair + 1) * rows], out)
    return out


def matmul(a, b):
    return jnp.dot(a, b, preferred_element_type=F32)


def own_half(out, group_size):
    tok = out.shape[1] // 2
    return jnp.concatenate([out[:group_size, :tok], out[group_size:, tok:]], axis=0)


def pair_product(x, table, group_size):
    return own_half(matmul(x, table), group_size)


def turned(row, size):
    ring = pltpu.roll(jnp.broadcast_to(row, (size, size)), 0, 1, stride=1, stride_axis=0)
    return ring.astype(BF16)


def series(x):
    out = jnp.ones_like(x)
    for n in range(TERMS, 1, -1):
        out = 1.0 - x / n * out
    return out


def tile_of(i):
    return pl.ds(pl.multiple_of(i * LANES, LANES), LANES)


def spans(channels):
    size = max(2 * LANES, channels // PARTS)
    return [pl.ds(start, size) for start in range(0, channels, size)]


def gated(k, v, out_ref):
    for start in range(0, out_ref.shape[0], LANES):
        at = pl.ds(start, LANES)
        out_ref[at, :] = (k[:, at].astype(F32) * v[:, at].astype(F32)).astype(BF16).T


def first_kernel(k_hbm, v_hbm, out_ref, *refs):
    later, (k_ref, v_ref, sems) = refs[:-3], refs[-3:]
    chunk = out_ref.shape[0]
    copies = []
    for n, to in enumerate((k_ref, v_ref) + later):
        source = (k_hbm, v_hbm)[n % 2].at[:, pl.ds(0, chunk) if n < 2 else pl.ds(chunk, to.shape[1])]
        copies.append(pltpu.make_async_copy(source, to, sems.at[n]))
        copies[-1].start()
    copies[0].wait()
    copies[1].wait()
    gated(k_ref, v_ref, out_ref)
    for copy in copies[2:]:
        copy.wait()


def prep_kernel(
    group_size, bits, place_ref, u_refs, gain_hbm, taps_hbm, rate_hbm, residue_hbm, resid_hbm, q_hbm, k_hbm,
    base_ref, gate_ref, key_ref, upper_ref, impulse, leave_ref, entry_ref, factor_ref, keep_ref, take_ref,
    taps, rates, weights, lower_ref,
    gain_ref, taps_ref, rate_ref, residue_ref, resid_ref, q_ref, k_ref, sems,
):
    tok = u_refs[0].shape[1]
    channels = sum(ref.shape[0] for ref in u_refs)
    poles, groups = rate_ref.shape
    per, width = LANES // group_size, 2 * group_size
    sources = (taps_hbm, rate_hbm, residue_hbm, gain_hbm, resid_hbm, q_hbm, k_hbm)
    places = (taps_ref, rate_ref, residue_ref, gain_ref, resid_ref, q_ref, k_ref)
    copies = [pltpu.make_async_copy(a, b, sems.at[n]) for n, (a, b) in enumerate(zip(sources, places))]
    for copy in copies:
        copy.start()
    row = lax.broadcasted_iota(jnp.int32, (tok, tok), 0)
    col = lax.broadcasted_iota(jnp.int32, (tok, tok), 1)
    causal = jnp.where(row <= col, 1.0, 0.0).astype(BF16)
    live = jnp.where(place_ref[0] > 0, 1.0, 0.0)
    future = jnp.where(row <= col, 0.0, live).astype(BF16)

    copies[0].wait()
    taps[...] = taps_ref[...].astype(F32)

    def taps_tables(i, _):
        for k in range(SPAN):
            ring = turned(taps[pl.ds(i * SPAN + k, 1), :], tok)
            at, cols = i * (SPAN // 2) + k // 2, pl.ds(k % 2 * tok, tok)
            lower_ref[at, :, cols] = ring * causal
            upper_ref[at, :, cols] = ring * future
        return 0

    lax.fori_loop(0, groups // SPAN, taps_tables, 0)

    copies[1].wait()
    copies[2].wait()
    twice = 2.0 * rate_ref[...]
    weight = residue_ref[...] * jnp.sqrt(jnp.where(twice < SMALL, twice * series(twice), 1.0 - jnp.exp(-twice)))
    for g in range(groups):
        at = pl.ds(g * poles, poles)
        rates[at, :] = jnp.broadcast_to(rate_ref[:, g : g + 1], (poles, tok))
        weights[at, :] = jnp.broadcast_to(weight[:, g : g + 1], (poles, tok))

    position = lax.broadcasted_iota(jnp.int32, (poles, tok), 1)
    now = position.astype(F32)
    ahead = (position + 1).astype(F32)
    remain = (tok - 1 - position).astype(F32)
    place = place_ref[0]
    lane_of = lane_group((poles, LANES), group_size)

    def decays(i, _):
        spread = jnp.zeros((poles, LANES), F32)
        for k in range(per):
            at = pl.ds(pl.multiple_of((i * per + k) * poles, poles), poles)
            rate, weight = rates[at, :], weights[at, :]
            impulse[pl.ds(i * per + k, 1), :] = jnp.sum(weight * jnp.exp(-rate * now), axis=0, keepdims=True)
            leave_ref[i, pl.ds(k // 2 * poles, poles), pl.ds(k % 2 * tok, tok)] = jnp.exp(-rate * remain)
            weights[at, :] = weight * jnp.exp(-rate * ahead)
            spread = jnp.where(lane_of == k, rate, spread)
        spread = spread * tok
        at = tile_of(i)
        for step, bit in enumerate(bits):
            late = (place & bit) != 0
            behind = (place & (bit - 1)).astype(F32)
            whole = jnp.exp(-spread * bit)
            factor_ref[step, :, at] = jnp.where(late, jnp.exp(-spread * behind), 0.0)
            keep_ref[step, :, at] = jnp.where(late, 1.0, whole)
            take_ref[step, :, at] = jnp.where(late, whole, 1.0)
        return 0

    lax.fori_loop(0, channels // LANES, decays, 0, unroll=2)

    for pair in range(channels // width):
        at = pl.ds(pair * width, width)
        base_ref[at, :] = pair_product(rows_of(u_refs, pair * width, width), lower_ref[pair], group_size)

    for copy in copies[3:]:
        copy.wait()
    for i in range(channels // LANES):
        at = pl.ds(i * LANES, LANES)
        gate = q_ref[:, at].T.astype(F32)
        gate_ref[at, :] = gate
        base_ref[at, :] = resid_ref[:, at].T.astype(F32) + gate * base_ref[at, :]
        key_ref[at, :] = (k_ref[:, at].astype(F32) * gain_ref[i : i + 1, :].astype(F32)).T
        enter = weights[pl.ds(i * per * poles, per * poles), :]
        entry_ref[i // 2, :, pl.ds(i % 2 * per * poles, per * poles)] = enter.T.astype(BF16)


def square_kernel(impulse_ref, square_ref):
    groups, tok = impulse_ref.shape
    row = lax.broadcasted_iota(jnp.int32, (tok, tok), 0)
    col = lax.broadcasted_iota(jnp.int32, (tok, tok), 1)
    causal = jnp.where(row <= col, 1.0, 0.0).astype(BF16)

    def body(i, _):
        for k in range(SPAN):
            ring = turned(impulse_ref[pl.ds(i * SPAN + k, 1), :], tok)
            square_ref[i * (SPAN // 2) + k // 2, :, pl.ds(k % 2 * tok, tok)] = ring * causal
        return 0

    lax.fori_loop(0, groups // SPAN, body, 0)


def mix_kernel(group_size, first, halo_ref, upper_ref, base_ref, gate_ref, key_ref, *refs):
    before, (mixed_ref, z_ref, sum_ref) = refs[:-3], refs[-3:]
    channels, tok = halo_ref.shape
    width = 2 * group_size
    total = jnp.zeros((width, tok), F32)
    for pair in range(channels // width):
        at, there = pl.ds(pair * width, width), pl.ds(first + pair * width, width)
        past = pair_product(halo_ref[at, :], upper_ref[first // width + pair], group_size)
        mixed = (base_ref[there, :] + gate_ref[there, :] * past).astype(BF16)
        mixed_ref[at, :] = mixed
        mixed = mixed.astype(F32)
        z_ref[at, :] = key_ref[there, :] * mixed
        total = total + mixed * mixed
    total = jnp.sum(total, axis=0, keepdims=True)
    for ref in before:
        total = total + ref[...]
    sum_ref[...] = total


def rows_of(refs, start, size):
    for ref in refs:
        if start < ref.shape[0]:
            return ref[pl.ds(start, size), :]
        start -= ref.shape[0]


def turn_kernel(group_size, z_refs, zb_ref):
    for i in range(zb_ref.shape[0]):
        zb_ref[i] = by_parity(rows_of(z_refs, i * LANES, LANES).astype(BF16).T, group_size)


def written(tile, width, out_hbm, out_ref, sem):
    copies = []
    for n, part in enumerate(spans(out_ref.shape[1])):
        for start in range(part.start, part.start + part.size, width):
            out_ref[:, pl.ds(start, width)] = tile(start // width)
        copies.append(pltpu.make_async_copy(out_ref.at[:, part], out_hbm.at[:, part], sem.at[n]))
        copies[-1].start()
    for copy in copies:
        copy.wait()


def out_kernel(mixed_refs, out_hbm, out_ref, sem):
    written(lambda i: rows_of(mixed_refs, i * LANES, LANES).T, LANES, out_hbm, out_ref, sem)


def state_kernel(group_size, width, parts, *refs):
    sums, (leave_ref, zb_ref, state_ref, sent_ref, scale_ref) = refs[:parts], refs[parts:]
    square_sum = sums[0][...]
    for other in sums[1:]:
        square_sum = square_sum + other[...]
    scale = lax.rsqrt(square_sum / width + 1e-06)
    scale_ref[...] = scale
    twice = jnp.concatenate([scale, scale], axis=1)
    for i in range(leave_ref.shape[0]):
        at = pl.ds(i * LANES, LANES)
        leaving = (leave_ref[i] * twice).astype(BF16)
        state = own_lanes(matmul(leaving, zb_ref[i]), group_size)
        state_ref[:, at] = state
        sent_ref[:, at] = state.astype(BF16)


def local_kernel(group_size, scale_ref, z_refs, square_ref, local_ref):
    width = 2 * group_size
    scale = scale_ref[...]
    first = 0
    for z_ref in z_refs:

        def body(i, _, z_ref=z_ref, first=first):
            rows = []
            for pair in range(LANES // width):
                at = pl.ds(pl.multiple_of(i * LANES + pair * width, width), width)
                y = z_ref[at, :] * scale
                high = y.astype(BF16)
                low = (y - high.astype(F32)).astype(BF16)
                table = square_ref[(first + i * LANES) // width + pair]
                out = matmul(jnp.concatenate([high, low], axis=0), table)
                rows.append(own_half(out[:width] + out[width:], group_size))
            local_ref[:, tile_of(first // LANES + i)] = jnp.concatenate(rows, axis=0).T
            return 0

        lax.fori_loop(0, z_ref.shape[0] // LANES, body, 0, unroll=4)
        first += z_ref.shape[0]


def final_kernel(group_size, rounds, *refs):
    got, (factor_ref, entry_ref, local_ref, q_ref, out_hbm, out_ref, sem) = refs[:rounds], refs[rounds:]
    poles, _ = got[0].shape
    per = LANES // group_size
    group_of = lane_group((poles, LANES), group_size)
    empty = jnp.zeros((per * poles, LANES), BF16)
    masks = [jnp.where(group_of == g, 1.0, 0.0).astype(BF16) for g in range(per)]

    def spread(i):
        at = pl.ds(i * LANES, LANES)
        carried = factor_ref[0, :, at] * got[0][:, at].astype(F32)
        for step in range(1, rounds):
            carried = carried + factor_ref[step, :, at] * got[step][:, at].astype(F32)
        carried = carried.astype(BF16)
        return jnp.concatenate([carried * mask for mask in masks], axis=0)

    def tile(i):
        at = pl.ds(2 * i * LANES, 2 * LANES)
        left = jnp.concatenate([spread(2 * i), empty], axis=1)
        right = jnp.concatenate([empty, spread(2 * i + 1)], axis=1)
        conv = local_ref[:, at] + matmul(entry_ref[i], jnp.concatenate([left, right], axis=0))
        return (q_ref[:, at].astype(F32) * conv).astype(BF16)

    written(tile, 2 * LANES, out_hbm, out_ref, sem)


def held(shape, dtype):
    return jax.ShapeDtypeStruct(shape, dtype)


def call(kernel, outs, scratch, flops, *args, **more):
    places = more.get("in_specs", [VMEM] * len(args))
    args = [pltpu.with_memory_space_constraint(a, pltpu.HBM) if s is HBM else a for a, s in zip(args, places)]
    specs = [[s] * len(a) if isinstance(a, list) else s for a, s in zip(args, places)]
    size = sum(a.size * a.dtype.itemsize for a in jax.tree.leaves(args))
    return pl.pallas_call(
        kernel,
        in_specs=specs,
        out_specs=more.get("out_specs", jax.tree.map(lambda _: VMEM, outs)),
        out_shape=outs,
        scratch_shapes=scratch,
        cost_estimate=pl.CostEstimate(flops=flops, bytes_accessed=size, transcendentals=0),
        compiler_params=pltpu.CompilerParams(vmem_limit_bytes=GRANT),
    )(*args)


def per_device(resid, q_mr, k_mr, v_mr, mr_taps, norm_gain, q_lr, k_lr, pole_rate, residue):
    tok, channels = resid.shape
    groups, tap_count = mr_taps.shape
    poles = pole_rate.shape[0]
    group_size = channels // groups
    assert tap_count == tok and channels % (16 * LANES) == 0 and LANES % (2 * group_size) == 0
    tiles, per = channels // LANES, LANES // group_size
    shards = lax.axis_size("ctx")
    bits = [1 << b for b in range((shards - 1).bit_length())]
    rounds = len(bits)
    place = lax.axis_index("ctx").astype(jnp.int32).reshape(1)
    work = 4 * tok * tok * channels

    sizes = [channels * FIRST // 16, channels - channels * FIRST // 16]
    firsts = [0, sizes[0]]
    rows = pltpu.VMEM((tok, channels), BF16)
    part = pltpu.VMEM((tok, sizes[0]), BF16)
    sem = pltpu.SemaphoreType.DMA((PARTS,))
    u0, k1, v1 = call(
        first_kernel, [held((sizes[0], tok), BF16)] + [held((tok, sizes[1]), BF16)] * 2,
        [part, part, pltpu.SemaphoreType.DMA((4,))], work // 8, k_mr, v_mr, in_specs=[HBM, HBM],
    )
    halo = [passed_on(u0, True)]
    u = [u0, call(gated, held((sizes[1], tok), BF16), [], work // 8, k1, v1)]
    halo.append(passed_on(u[1], False))

    tall = held((channels, tok), F32)
    table = held((groups // 2, tok, 2 * tok), BF16)
    steps = held((rounds, poles, channels), F32)
    base, gate, key, upper, impulse, leave, entry, factor, keep, take = call(
        functools.partial(prep_kernel, group_size, bits),
        (
            tall, tall, tall, table, held((groups, tok), F32),
            held((tiles, per // 2 * poles, 2 * tok), F32),
            held((tiles // 2, tok, 2 * per * poles), BF16),
            steps, steps, steps,
        ),
        [
            pltpu.VMEM((groups, tok), F32), pltpu.VMEM((groups * poles, tok), F32),
            pltpu.VMEM((groups * poles, tok), F32), pltpu.VMEM(table.shape, BF16), pltpu.VMEM((tiles, LANES), BF16),
            pltpu.VMEM((groups, tok), BF16), pltpu.VMEM((poles, groups), F32), pltpu.VMEM((poles, groups), F32),
            rows, rows, rows, pltpu.SemaphoreType.DMA((7,)),
        ],
        8 * work,
        place, u, norm_gain.reshape(tiles, LANES), mr_taps, pole_rate, residue, resid, q_mr, k_lr,
        in_specs=[SMEM, VMEM] + [HBM] * 7,
    )
    mixed_t, z, square_sum = [], [], []
    for first, past in zip(firsts, halo):
        outs = call(
            functools.partial(mix_kernel, group_size, first),
            (held(past.shape, BF16), held(past.shape, F32), held((1, tok), F32)),
            [],
            work // 2,
            past, upper, base, gate, key, *square_sum,
        )
        mixed_t.append(outs[0])
        z.append(outs[1])
        square_sum = [outs[2]]
    square_sum = square_sum[0]
    sums = everyone(square_sum, "tp")
    zb = call(
        functools.partial(turn_kernel, group_size), held((tiles, 2 * tok, LANES), BF16), [], work // 2, z
    )
    small = (poles, channels)
    state, sent, scale = call(
        functools.partial(state_kernel, group_size, channels * lax.axis_size("tp"), len(sums)),
        (held(small, F32), held(small, BF16), held((1, tok), F32)),
        [],
        work // 8,
        *sums, leave, zb,
    )
    square = call(square_kernel, table, [], work, impulse)
    local = call(
        functools.partial(local_kernel, group_size),
        held((tok, channels), F32),
        [],
        work,
        scale, z, square,
    )
    got = []
    for step, bit in enumerate(bits):
        got.append(swapped(sent, "ctx", bit))
        state = keep[step] * state + take[step] * got[step].astype(F32)
        sent = state.astype(BF16)
    mixed = call(out_kernel, held((tok, channels), BF16), [rows, sem], work // 4, mixed_t, out_specs=HBM)
    lr_out = call(
        functools.partial(final_kernel, group_size, rounds),
        held((tok, channels), BF16),
        [rows, sem],
        work // 8,
        *got, factor, entry, local, q_lr,
        out_specs=HBM,
    )
    return (mixed, lr_out)


def solution(mesh):
    whole, tables = P("ctx", "tp"), P(None, "tp")
    placed = (whole,) * 4 + (P("tp", None), P("tp")) + (whole,) * 2 + (tables,) * 2
    return jax.shard_map(per_device, mesh=mesh, in_specs=placed, out_specs=(whole, whole), check_vma=False)
```
